32 devices in a mesh: dp: 32 (over z, y, x, core).
Axes of the slice: x: 2, y: 2, z: 4, core: 2. Of those that a mesh axis runs over, the one named last changes fastest.
Arguments:
- tokens: float32 [64, 197, 384], P('dp'), may hold values from -6 to 6
- params: float32 [1774080], P('dp'), as said below
- moment1: float32 [1774080], P('dp'), may hold values from -0.0625 to 0.0625
- moment2: float32 [1774080], P('dp'), may hold values from 1e-06 to 1e-05
- cotangent: float32 [64, 197, 384], P('dp'), may hold values from -6 to 6
Outputs:
- result: float32 [64, 197, 384], P('dp')
- grad_tokens: float32 [64, 197, 384], P('dp')
- grad_params: float32 [1774080], P('dp')
- new_params: float32 [1774080], P('dp')
- new_moment1: float32 [1774080], P('dp')
- new_moment2: float32 [1774080], P('dp')
The draws below stay inside these ranges and needn't reach their ends.
Inputs may be any that keep to these rules, and one draw needn't show every extreme that they name: `params`: finite floats.
All inputs are finite; a program needn't handle non-finite values.
Results may differ from the reference program's by a relative error of at most 0.0071.
The reference program's roundings to bfloat16 on the way count: a program that leaves them out, or rounds other values in their place, can miss the bound.
Values may be sent and summed in bfloat16 or wider, within the bound.
A program may use at most 128 MiB of HBM per device.

```python
import math
import jax
import jax.numpy as jnp
from jax import lax

D = 384
HEADS = 6
FF = 1536
SEQ = 197
IMG_MB = 1
STEP = 3
IMAGES = 64
TOKENS = 12608
NPARAM = 1774080


def draw_params(key, part):
    keys = jax.random.split(key, 6)
    w_qkv = jax.random.normal(keys[0], (D, 3 * D), jnp.float32) * D ** (-0.5)
    w_out = jax.random.normal(keys[1], (D, D), jnp.float32) * (3.2 * D ** (-0.5))
    w_up = jax.random.normal(keys[2], (D, FF), jnp.float32) * D ** (-0.5)
    w_down = jax.random.normal(keys[3], (FF, D), jnp.float32) * FF ** (-0.5)
    spread = jax.random.normal(keys[4], (8, D), jnp.float32)
    gain_rows = jnp.array([1.0, 0.0, 0.0, 0.0, 0.0, 1.0, 0.0, 0.0], jnp.float32)[:, None]
    spread_rows = jnp.array([0.1, 0.3, 0.3, 0.3, 0.3, 0.1, 0.3, 0.3], jnp.float32)[:, None]
    vectors = gain_rows + spread_rows * spread
    up_bias = jax.random.normal(keys[5], (FF,), jnp.float32) * 0.3
    return jnp.concatenate([w_qkv.reshape(-1), w_out.reshape(-1), w_up.reshape(-1), w_down.reshape(-1), vectors.reshape(-1), up_bias])


def block_scale(key, dims, pieces, low, largest):
    factor_of = 1.0
    for axis_at, blocks in pieces:
        steps = jax.random.uniform(jax.random.fold_in(jax.random.fold_in(key, 6), axis_at), (blocks,), jnp.float32, low / len(pieces), largest / len(pieces))
        factor_of = factor_of * jnp.repeat(jnp.exp(steps), dims[axis_at] // blocks).reshape((-1,) + (1,) * (len(dims) - 1 - axis_at))
    return factor_of


def centred(own_key, shape, scale, bound, pieces=(), kind=jnp.bfloat16):
    values = scale * jax.random.normal(own_key, shape, jnp.float32)
    if pieces:
        values = values * block_scale(own_key, shape, pieces, -0.22, 0.18)
    return jnp.clip(values, -bound, bound).astype(kind)


def setup_inputs(seed: int = 0) -> dict:
    seeds = jax.random.split(jax.random.key(seed), 6)
    return {
        "tokens": centred(seeds[0], (IMAGES, SEQ, D), 1.0, 6.0, ((0, 32),), jnp.float32),
        "params": draw_params(jax.random.fold_in(seeds[5], 71), 0),
        "moment1": centred(seeds[2], (NPARAM,), 0.01, 0.0625, ((0, 32),), jnp.float32),
        "moment2": jnp.clip(jnp.exp(math.log(9.999999747378752e-06) - 2.3025851 * jax.random.uniform(seeds[3], (NPARAM,), jnp.float32) ** block_scale(seeds[3], (NPARAM,), ((0, 32),), -0.2, 0.2)), 9.999999974752427e-07, 9.999999747378752e-06),
        "cotangent": centred(seeds[4], (IMAGES, SEQ, D), 1.0, 6.0, ((0, 32),), jnp.float32),
    }


def product(spec, left, right):
    return jnp.einsum(spec, left.astype(jnp.float32), right.astype(jnp.float32), precision=lax.Precision.HIGHEST)

def token_sum(left, right):
    return lax.dot_general(left, right, (((0,), (0,)), ((), ())), preferred_element_type=jnp.float32)

def times_t(left, right):
    return lax.dot_general(left, right, (((1,), (1,)), ((), ())), preferred_element_type=jnp.float32)

def layer_norm(values):
    center = values - lax.optimization_barrier(jnp.mean(values, axis=-1, keepdims=True))
    factor = lax.rsqrt(lax.optimization_barrier(jnp.mean(center * center, axis=-1, keepdims=True)) + 1e-06)
    return (center * factor, factor)

def norm_back(grad_hat, normed, factor):
    return factor * (grad_hat - lax.optimization_barrier(jnp.mean(grad_hat, axis=-1, keepdims=True)) - normed * lax.optimization_barrier(jnp.mean(grad_hat * normed, axis=-1, keepdims=True)))

def unpack(flat):
    first = 3 * D * D
    second = first + D * D
    third = second + D * FF
    fourth = third + FF * D
    fifth = fourth + 8 * D
    return (flat[:first].reshape(D, 3 * D), flat[first:second].reshape(D, D), flat[second:third].reshape(D, FF), flat[third:fourth].reshape(FF, D), flat[fourth:fifth].astype(jnp.float32).reshape(8, D), flat[fifth:].astype(jnp.float32))

def forward(tokens_mb, weights):
    w_qkv, w_out, w_up, w_down, vectors, up_bias = weights
    batch, length, width = tokens_mb.shape
    normed_in, scale_in = layer_norm(tokens_mb)
    attn_input = (normed_in * vectors[0] + vectors[1]).astype(jnp.bfloat16).reshape(-1, width)
    projected = jnp.dot(attn_input, w_qkv, preferred_element_type=jnp.float32)
    heads_shape = (batch, length, HEADS, width // HEADS)
    query_half = (projected[:, :width] + vectors[2]).astype(jnp.bfloat16).reshape(heads_shape)
    key_half = projected[:, width:2 * width].astype(jnp.bfloat16).reshape(heads_shape)
    value_half = (projected[:, 2 * width:] + vectors[3]).astype(jnp.bfloat16).reshape(heads_shape)
    scores = product('bqhe,bkhe->bhqk', query_half, key_half) * (width // HEADS) ** (-0.5)
    top = lax.optimization_barrier(jnp.max(scores, axis=-1, keepdims=True))
    raw_weights = jnp.exp(scores - top)
    total = lax.optimization_barrier(jnp.sum(raw_weights, axis=-1, keepdims=True))
    log_total = top + jnp.log(total)
    probs = (raw_weights / total).astype(jnp.bfloat16)
    context = product('bhqk,bkhe->bqhe', probs, value_half).astype(jnp.bfloat16).reshape(-1, width)
    hidden_mid = tokens_mb + (jnp.dot(context, w_out, preferred_element_type=jnp.float32) + vectors[4]).reshape(tokens_mb.shape)
    normed_mid, scale_mid = layer_norm(hidden_mid)
    mlp_input = (normed_mid * vectors[5] + vectors[6]).astype(jnp.bfloat16).reshape(-1, width)
    pre_act = jnp.dot(mlp_input, w_up, preferred_element_type=jnp.float32) + up_bias
    activated = jax.nn.gelu(pre_act, approximate=False).astype(jnp.bfloat16)
    result = hidden_mid + (jnp.dot(activated, w_down, preferred_element_type=jnp.float32) + vectors[7]).reshape(tokens_mb.shape)
    saved = (normed_in, scale_in, attn_input, query_half, key_half, value_half, log_total, context, normed_mid, scale_mid, mlp_input, pre_act, activated)
    return (result, saved)

def backward(saved, grad_result, weights):
    w_qkv, w_out, w_up, w_down, vectors, up_bias = weights
    normed_in, scale_in, attn_input, query_half, key_half, value_half, log_total, context, normed_mid, scale_mid, mlp_input, pre_act, activated = saved
    width = grad_result.shape[-1]
    grad_flat = grad_result.reshape(-1, width)
    grad_half = grad_flat.astype(jnp.bfloat16)
    grad_down = token_sum(activated, grad_half)
    grad_act = times_t(grad_half, w_down)
    slope = 0.5 * (1.0 + jax.scipy.special.erf(pre_act * 0.7071067811865476)) + pre_act * jnp.exp(-0.5 * pre_act * pre_act) * 0.3989422804014327
    grad_pre = grad_act * slope
    grad_pre_half = grad_pre.astype(jnp.bfloat16)
    grad_up = token_sum(mlp_input, grad_pre_half)
    grad_mlp_in = times_t(grad_pre_half, w_up)
    mid_flat = normed_mid.reshape(-1, width)
    grad_hidden = grad_result + norm_back((grad_mlp_in * vectors[5]).reshape(grad_result.shape), normed_mid, scale_mid)
    hidden_flat = grad_hidden.reshape(-1, width)
    hidden_half = hidden_flat.astype(jnp.bfloat16)
    grad_wout = token_sum(context, hidden_half)
    grad_context = times_t(hidden_half, w_out).astype(jnp.bfloat16).reshape(query_half.shape)
    scale_factor = (width // HEADS) ** (-0.5)
    scores = product('bqhe,bkhe->bhqk', query_half, key_half) * scale_factor
    probs_full = jnp.exp(scores - log_total)
    probs_half = probs_full.astype(jnp.bfloat16)
    grad_value = product('bhqk,bqhe->bkhe', probs_half, grad_context)
    grad_probs = product('bqhe,bkhe->bhqk', grad_context, value_half)
    delta = lax.optimization_barrier(jnp.sum(probs_full * grad_probs, axis=-1, keepdims=True))
    grad_scores = (probs_full * (grad_probs - delta) * scale_factor).astype(jnp.bfloat16)
    grad_query = product('bhqk,bkhe->bqhe', grad_scores, key_half).reshape(-1, width)
    grad_key = product('bhqk,bqhe->bkhe', grad_scores, query_half).reshape(-1, width)
    grad_value = grad_value.reshape(-1, width)
    proj_half = jnp.concatenate([grad_query, grad_key, grad_value], axis=1).astype(jnp.bfloat16)
    grad_wqkv = token_sum(attn_input, proj_half)
    grad_attn_in = times_t(proj_half, w_qkv)
    in_flat = normed_in.reshape(-1, width)
    grad_tokens = grad_hidden + norm_back((grad_attn_in * vectors[0]).reshape(grad_result.shape), normed_in, scale_in)
    vector_grads = jnp.stack([lax.optimization_barrier(jnp.sum(grad_attn_in * in_flat, axis=0)), lax.optimization_barrier(jnp.sum(grad_attn_in, axis=0)), lax.optimization_barrier(jnp.sum(grad_query, axis=0)), lax.optimization_barrier(jnp.sum(grad_value, axis=0)), lax.optimization_barrier(jnp.sum(hidden_flat, axis=0)), lax.optimization_barrier(jnp.sum(grad_mlp_in * mid_flat, axis=0)), lax.optimization_barrier(jnp.sum(grad_mlp_in, axis=0)), lax.optimization_barrier(jnp.sum(grad_flat, axis=0))])
    flat = jnp.concatenate([grad_wqkv.reshape(-1), grad_wout.reshape(-1), grad_up.reshape(-1), grad_down.reshape(-1), vector_grads.reshape(-1), lax.optimization_barrier(jnp.sum(grad_pre, axis=0))])
    return (grad_tokens, flat)

def adamw(params, grads, first, second, position):
    first_end = 3 * D * D
    second_end = first_end + D * D
    third_end = second_end + D * FF
    fourth_end = third_end + FF * D
    rate = jnp.where(position < first_end, 0.01, jnp.where(position < second_end, 0.1, jnp.where(position < third_end, 0.01, jnp.where(position < fourth_end, 0.005, 0.1))))
    first_new = 0.9 * first + 0.1 * grads
    second_new = 0.999 * second + 0.001 * grads * grads
    update = first_new / (1.0 - 0.9 ** STEP) / (jnp.sqrt(second_new / (1.0 - 0.999 ** STEP)) + 1e-08) + 0.1 * params
    return (params - rate * update, first_new, second_new)

def reference(tokens, params, moment1, moment2, cotangent):
    weights = unpack(params.astype(jnp.bfloat16))
    blocks = tokens.reshape(-1, IMG_MB, SEQ, D)
    grad_blocks = cotangent.reshape(-1, IMG_MB, SEQ, D)

    def one_block(total, items):
        block, grad_block = items
        result, saved = forward(block, weights)
        grad_in, flat = backward(saved, grad_block, weights)
        return (total + flat, (result, grad_in))
    total, (results, grads_in) = lax.scan(one_block, jnp.zeros(params.shape, jnp.float32), (blocks, grad_blocks))
    grad_params = total * (1.0 / math.sqrt(TOKENS))
    position = jnp.arange(params.shape[0], dtype=jnp.int32)
    new_params, new_first, new_second = adamw(params, grad_params, moment1, moment2, position)
    return (results.reshape(tokens.shape), grads_in.reshape(tokens.shape), grad_params, new_params, new_first, new_second)
```

```python
import math

import jax
import jax.numpy as jnp
from jax import lax
from jax.experimental import pallas as pl
from jax.experimental.pallas import tpu as pltpu
import functools
from jax.sharding import PartitionSpec as P

D = 384
HEADS = 6
FF = 1536
SEQ = 197
STEP = 3


LANES = 128
LINES = 4 * 1152 + 12


def plan(devices, share):
    bits = devices.bit_length() - 1
    rows = -(-(share + D - 1) // D)
    rows = -(-rows // 32) * 32
    far = list(range(bits - 1, 2, -1))
    orders = [far + [1, 2, 0], far + [2, 1, 0]]
    half = rows // 2
    if half % 16 == 0 and half > 16:
        first = -(-half // 2 // 16) * 16
        sizes = [first, first, half - first, half - first]
    else:
        sizes = [half, half]
    parts = []
    start = 0
    for index, size in enumerate(sizes):
        parts.append((start, size, orders[index % 2]))
        start += size
    return bits, rows, parts


def place(device, order):
    spot = 0
    for index, bit in enumerate(order):
        spot = spot + ((device // 2**bit) % 2) * 2**index
    return spot


def other(device, bit):
    step = 2**bit
    return device + step - 2 * step * ((device // step) % 2)


def greet(me, bits):
    barrier = pltpu.get_barrier_semaphore()
    for bit in range(bits):
        pl.semaphore_signal(
            barrier, inc=1, device_id=(other(me, bit),), device_id_type=pl.DeviceIdType.MESH
        )
    pl.semaphore_wait(barrier, bits)


def gather_kernel(devices, share, shard, w_qkv, w_out, w_up, w_down, tail, lines, *rest):
    bits, rows, parts = plan(devices, share)
    slots = rest[: len(parts)]
    local_sem, send_sem, recv_sem = rest[len(parts) :]
    me = lax.axis_index("dp")
    own = []
    for index, (start, size, order) in enumerate(parts):
        copy = pltpu.make_async_copy(
            shard.at[pl.ds(start, size)], slots[index].at[place(me, order)], local_sem.at[index]
        )
        copy.start()
        own.append(copy)
    greet(me, bits)
    for copy in own:
        copy.wait()
    waiting = [None] * len(parts)
    for stage in range(bits):
        for index, (start, size, order) in enumerate(parts):
            if waiting[index] is not None:
                waiting[index].wait()
            block = 2**stage
            begin = (place(me, order) // block) * block
            piece = slots[index].at[pl.ds(begin, block)]
            copy = pltpu.make_async_remote_copy(
                src_ref=piece,
                dst_ref=piece,
                send_sem=send_sem.at[index, stage],
                recv_sem=recv_sem.at[index, stage],
                device_id=(other(me, order[stage]),),
                device_id_type=pl.DeviceIdType.MESH,
            )
            copy.start()
            waiting[index] = copy
    for copy in waiting:
        copy.wait()
    chunks = D // LANES
    for device in range(devices):
        first = device * share // D
        shared = device * share % D != 0
        for index, (start, size, order) in enumerate(parts):
            spot = place(device, order)
            at = first + start
            for chunk in range(chunks):
                if start == 0 and shared:
                    before = lines[chunk, at : at + 1, :]
                lines[chunk, at : at + size, :] = slots[index][
                    spot, :, chunk * LANES : (chunk + 1) * LANES
                ].astype(jnp.float32)
                if start == 0 and shared:
                    lines[chunk, at : at + 1, :] = lines[chunk, at : at + 1, :] + before
    spread(lines, 0, w_qkv, 3)
    spread(lines, 1152, w_out, 1)
    spread(lines, 1536, w_up, 4)
    spread(lines, 3072, w_down, 1)
    spread(lines, 4608, tail, 1)


def spread(lines, first, out, times):
    height = out.shape[0]
    for column in range(times):
        for chunk in range(D // LANES):
            if times == 1:
                value = lines[chunk, first : first + height, :]
            else:
                value = lines[chunk, pl.ds(first + column, height, stride=times), :]
            at = column * D + chunk * LANES
            out[:, at : at + LANES] = value.astype(out.dtype)


def gather_weights(params, devices):
    share = params.shape[0]
    bits, rows, parts = plan(devices, share)
    offset = (lax.axis_index("dp") * share) % D
    flat = jnp.zeros((rows * D,), jnp.float32)
    flat = lax.dynamic_update_slice(flat, params, (offset,))
    shard = flat.reshape(rows, D).astype(jnp.bfloat16)
    vmem = pl.BlockSpec(memory_space=pltpu.VMEM)
    return pl.pallas_call(
        functools.partial(gather_kernel, devices, share),
        out_shape=(
            jax.ShapeDtypeStruct((D, 3 * D), jnp.bfloat16),
            jax.ShapeDtypeStruct((D, D), jnp.bfloat16),
            jax.ShapeDtypeStruct((D, FF), jnp.bfloat16),
            jax.ShapeDtypeStruct((FF, D), jnp.bfloat16),
            jax.ShapeDtypeStruct((16, D), jnp.float32),
        ),
        in_specs=[vmem],
        out_specs=[vmem] * 5,
        scratch_shapes=[pltpu.VMEM((D // LANES, LINES + rows + 24, LANES), jnp.float32)]
        + [pltpu.VMEM((devices, size, D), jnp.bfloat16) for _, size, _ in parts]
        + [
            pltpu.SemaphoreType.DMA((len(parts),)),
            pltpu.SemaphoreType.DMA((len(parts), bits)),
            pltpu.SemaphoreType.DMA((len(parts), bits)),
        ],
        compiler_params=pltpu.CompilerParams(
            collective_id=0, has_side_effects=True, vmem_limit_bytes=60 * 2**20
        ),
    )(shard)


def scatter_kernel(devices, share, g_qkv, g_out, g_up, g_down, g_tail, out, lines, *rest):
    bits, rows, parts = plan(devices, share)
    count = len(parts)
    slots, landed, sums = rest[:count], rest[count : 2 * count], rest[2 * count : 3 * count]
    send_sem, recv_sem = rest[3 * count :]
    me = lax.axis_index("dp")
    collect(lines, 0, g_qkv, 3)
    collect(lines, 1152, g_out, 1)
    collect(lines, 1536, g_up, 4)
    collect(lines, 3072, g_down, 1)
    collect(lines, 4608, g_tail, 1)
    lines[:, 4624:, :] = jnp.zeros_like(lines[:, 4624:, :])
    for device in range(devices):
        first = device * share // D
        for index, (start, size, order) in enumerate(parts):
            spot = place(device, order)
            at = first + start
            for chunk in range(D // LANES):
                slots[index][spot, :, chunk * LANES : (chunk + 1) * LANES] = lines[
                    chunk, at : at + size, :
                ].astype(jnp.bfloat16)
    greet(me, bits)
    waiting = [None] * count

    def send(index, stage):
        order = parts[index][2]
        block = 2**stage
        spot = place(me, order) // block
        away = spot + 1 - 2 * (spot % 2)
        copy = pltpu.make_async_remote_copy(
            src_ref=slots[index].at[pl.ds(away * block, block)],
            dst_ref=landed[index].at[pl.ds(block - 1, block)],
            send_sem=send_sem.at[index, stage],
            recv_sem=recv_sem.at[index, stage],
            device_id=(other(me, order[stage]),),
            device_id_type=pl.DeviceIdType.MESH,
        )
        copy.start()
        return copy

    for index in range(count):
        waiting[index] = send(index, bits - 1)
    for stage in range(bits - 1, -1, -1):
        for index, (start, size, order) in enumerate(parts):
            waiting[index].wait()
            block = 2**stage
            begin = (place(me, order) // block) * block
            if stage == 0:
                piece = sums[index][begin] if bits > 1 else slots[index][begin].astype(jnp.float32)
                out[start : start + size, :] = piece + landed[index][0].astype(jnp.float32)
                continue

            def add(step, carry, index=index, begin=begin, block=block, stage=stage):
                spot = begin + step
                if stage == bits - 1:
                    old = slots[index][spot].astype(jnp.float32)
                else:
                    old = sums[index][spot]
                new = old + landed[index][block - 1 + step].astype(jnp.float32)
                sums[index][spot] = new
                slots[index][spot] = new.astype(jnp.bfloat16)
                return carry

            lax.fori_loop(0, block, add, 0)
            waiting[index] = send(index, stage - 1)


def collect(lines, first, grads, times):
    height = grads.shape[0]
    for column in range(times):
        for chunk in range(D // LANES):
            at = column * D + chunk * LANES
            value = grads[:, at : at + LANES]
            if times == 1:
                lines[chunk, first : first + height, :] = value
            else:
                lines[chunk, pl.ds(first + column, height, stride=times), :] = value


def scatter_grads(grads, devices, share):
    bits, rows, parts = plan(devices, share)
    vmem = pl.BlockSpec(memory_space=pltpu.VMEM)
    total = pl.pallas_call(
        functools.partial(scatter_kernel, devices, share),
        out_shape=jax.ShapeDtypeStruct((rows, D), jnp.float32),
        in_specs=[vmem] * 5,
        out_specs=vmem,
        scratch_shapes=[pltpu.VMEM((D // LANES, LINES + rows + 24, LANES), jnp.float32)]
        + [pltpu.VMEM((devices, size, D), jnp.bfloat16) for _, size, _ in parts]
        + [pltpu.VMEM((devices, size, D), jnp.bfloat16) for _, size, _ in parts]
        + [pltpu.VMEM((devices, size, D), jnp.float32) for _, size, _ in parts]
        + [
            pltpu.SemaphoreType.DMA((len(parts), bits)),
            pltpu.SemaphoreType.DMA((len(parts), bits)),
        ],
        compiler_params=pltpu.CompilerParams(
            collective_id=1, has_side_effects=True, vmem_limit_bytes=63 * 2**20
        ),
    )(*grads)
    offset = (lax.axis_index("dp") * share) % D
    return lax.dynamic_slice(total.reshape(-1), (offset,), (share,))


def product(spec, left, right):
    return jnp.einsum(spec, left, right, preferred_element_type=jnp.float32)


def token_sum(left, right):
    return lax.dot_general(
        left, right, (((0,), (0,)), ((), ())), preferred_element_type=jnp.float32
    )


def times_t(left, right):
    return lax.dot_general(
        left, right, (((1,), (1,)), ((), ())), preferred_element_type=jnp.float32
    )


def layer_norm(values):
    center = values - jnp.mean(values, axis=-1, keepdims=True)
    factor = lax.rsqrt(jnp.mean(center * center, axis=-1, keepdims=True) + 1e-06)
    return (center * factor, factor)


def norm_back(grad_hat, normed, factor):
    return factor * (
        grad_hat
        - jnp.mean(grad_hat, axis=-1, keepdims=True)
        - normed * jnp.mean(grad_hat * normed, axis=-1, keepdims=True)
    )


def forward(tokens_mb, weights):
    w_qkv, w_out, w_up, w_down, vectors, up_bias = weights
    batch, length, width = tokens_mb.shape
    normed_in, scale_in = layer_norm(tokens_mb)
    attn_input = (normed_in * vectors[0] + vectors[1]).astype(jnp.bfloat16).reshape(-1, width)
    projected = jnp.dot(attn_input, w_qkv, preferred_element_type=jnp.float32)
    heads_shape = (batch, length, HEADS, width // HEADS)
    query_half = (projected[:, :width] + vectors[2]).astype(jnp.bfloat16).reshape(heads_shape)
    key_half = projected[:, width : 2 * width].astype(jnp.bfloat16).reshape(heads_shape)
    value_half = (projected[:, 2 * width :] + vectors[3]).astype(jnp.bfloat16).reshape(heads_shape)
    scores = product("bqhe,bkhe->bhqk", query_half, key_half) * (width // HEADS) ** (-0.5)
    top = jnp.max(scores, axis=-1, keepdims=True)
    raw_weights = jnp.exp(scores - top)
    total = jnp.sum(raw_weights, axis=-1, keepdims=True)
    log_total = top + jnp.log(total)
    probs = (raw_weights / total).astype(jnp.bfloat16)
    context = product("bhqk,bkhe->bqhe", probs, value_half).astype(jnp.bfloat16).reshape(-1, width)
    hidden_mid = tokens_mb + (
        jnp.dot(context, w_out, preferred_element_type=jnp.float32) + vectors[4]
    ).reshape(tokens_mb.shape)
    normed_mid, scale_mid = layer_norm(hidden_mid)
    mlp_input = (normed_mid * vectors[5] + vectors[6]).astype(jnp.bfloat16).reshape(-1, width)
    pre_act = jnp.dot(mlp_input, w_up, preferred_element_type=jnp.float32) + up_bias
    activated = jax.nn.gelu(pre_act, approximate=False).astype(jnp.bfloat16)
    result = hidden_mid + (
        jnp.dot(activated, w_down, preferred_element_type=jnp.float32) + vectors[7]
    ).reshape(tokens_mb.shape)
    saved = (
        normed_in,
        scale_in,
        attn_input,
        query_half,
        key_half,
        value_half,
        log_total,
        context,
        normed_mid,
        scale_mid,
        mlp_input,
        pre_act,
        activated,
    )
    return (result, saved)


def backward(saved, grad_result, weights):
    w_qkv, w_out, w_up, w_down, vectors, up_bias = weights
    (
        normed_in,
        scale_in,
        attn_input,
        query_half,
        key_half,
        value_half,
        log_total,
        context,
        normed_mid,
        scale_mid,
        mlp_input,
        pre_act,
        activated,
    ) = saved
    width = grad_result.shape[-1]
    grad_flat = grad_result.reshape(-1, width)
    grad_half = grad_flat.astype(jnp.bfloat16)
    grad_down = token_sum(activated, grad_half)
    grad_act = times_t(grad_half, w_down)
    slope = (
        0.5 * (1.0 + jax.scipy.special.erf(pre_act * 0.7071067811865476))
        + pre_act * jnp.exp(-0.5 * pre_act * pre_act) * 0.3989422804014327
    )
    grad_pre = grad_act * slope
    grad_pre_half = grad_pre.astype(jnp.bfloat16)
    grad_up = token_sum(mlp_input, grad_pre_half)
    grad_mlp_in = times_t(grad_pre_half, w_up)
    mid_flat = normed_mid.reshape(-1, width)
    grad_hidden = grad_result + norm_back(
        (grad_mlp_in * vectors[5]).reshape(grad_result.shape), normed_mid, scale_mid
    )
    hidden_flat = grad_hidden.reshape(-1, width)
    hidden_half = hidden_flat.astype(jnp.bfloat16)
    grad_wout = token_sum(context, hidden_half)
    grad_context = times_t(hidden_half, w_out).astype(jnp.bfloat16).reshape(query_half.shape)
    scale_factor = (width // HEADS) ** (-0.5)
    scores = product("bqhe,bkhe->bhqk", query_half, key_half) * scale_factor
    probs_full = jnp.exp(scores - log_total)
    probs_half = probs_full.astype(jnp.bfloat16)
    grad_value = product("bhqk,bqhe->bkhe", probs_half, grad_context)
    grad_probs = product("bqhe,bkhe->bhqk", grad_context, value_half)
    delta = jnp.sum(probs_full * grad_probs, axis=-1, keepdims=True)
    grad_scores = (probs_full * (grad_probs - delta) * scale_factor).astype(jnp.bfloat16)
    grad_query = product("bhqk,bkhe->bqhe", grad_scores, key_half).reshape(-1, width)
    grad_key = product("bhqk,bqhe->bkhe", grad_scores, query_half).reshape(-1, width)
    grad_value = grad_value.reshape(-1, width)
    proj_half = jnp.concatenate([grad_query, grad_key, grad_value], axis=1).astype(jnp.bfloat16)
    grad_wqkv = token_sum(attn_input, proj_half)
    grad_attn_in = times_t(proj_half, w_qkv)
    in_flat = normed_in.reshape(-1, width)
    grad_tokens = grad_hidden + norm_back(
        (grad_attn_in * vectors[0]).reshape(grad_result.shape), normed_in, scale_in
    )
    vector_grads = jnp.stack(
        [
            jnp.sum(grad_attn_in * in_flat, axis=0),
            jnp.sum(grad_attn_in, axis=0),
            jnp.sum(grad_query, axis=0),
            jnp.sum(grad_value, axis=0),
            jnp.sum(hidden_flat, axis=0),
            jnp.sum(grad_mlp_in * mid_flat, axis=0),
            jnp.sum(grad_mlp_in, axis=0),
            jnp.sum(grad_flat, axis=0),
        ]
    )
    tail = jnp.concatenate(
        [vector_grads, jnp.sum(grad_pre, axis=0).reshape(4, D), jnp.zeros((4, D), jnp.float32)]
    )
    return (grad_tokens, (grad_wqkv, grad_wout, grad_up, grad_down, tail))


def adamw(params, grads, first, second, position):
    first_end = 3 * D * D
    second_end = first_end + D * D
    third_end = second_end + D * FF
    fourth_end = third_end + FF * D
    rate = jnp.where(
        position < first_end,
        0.01,
        jnp.where(
            position < second_end,
            0.1,
            jnp.where(position < third_end, 0.01, jnp.where(position < fourth_end, 0.005, 0.1)),
        ),
    )
    first_new = 0.9 * first + 0.1 * grads
    second_new = 0.999 * second + 0.001 * grads * grads
    update = (
        first_new / (1.0 - 0.9**STEP) / (jnp.sqrt(second_new / (1.0 - 0.999**STEP)) + 1e-08)
        + 0.1 * params
    )
    return (params - rate * update, first_new, second_new)


def per_device(tokens, params, moment1, moment2, cotangent):
    devices = lax.axis_size("dp")
    length = params.shape[0]
    w_qkv, w_out, w_up, w_down, tail = gather_weights(params, devices)
    weights = (w_qkv, w_out, w_up, w_down, tail[:8], tail[8:12].reshape(FF))
    result, saved = forward(tokens, weights)
    grad_tokens, grads = backward(saved, cotangent, weights)
    shares = scatter_grads(grads, devices, length)
    count = tokens.shape[0] * tokens.shape[1] * devices
    grad_params = shares * (1.0 / math.sqrt(count))
    position = lax.axis_index("dp") * length + jnp.arange(length, dtype=jnp.int32)
    new_params, new_first, new_second = adamw(params, grad_params, moment1, moment2, position)
    return (result, grad_tokens, grad_params, new_params, new_first, new_second)


def solution(mesh):
    in_specs = (P("dp", None, None), P("dp"), P("dp"), P("dp"), P("dp", None, None))
    out_specs = (P("dp", None, None), P("dp", None, None), P("dp"), P("dp"), P("dp"), P("dp"))
    return jax.shard_map(
        per_device, mesh=mesh, in_specs=in_specs, out_specs=out_specs, check_vma=False
    )
```

```python
import math

import jax
import jax.numpy as jnp
from jax import lax
from jax.experimental import pallas as pl
from jax.experimental.pallas import tpu as pltpu
import functools
from jax.sharding import PartitionSpec as P

D = 384
HEADS = 6
FF = 1536
SEQ = 197
STEP = 3


LANES = 128
LINES = 4 * 1152 + 12


def plan(devices, share):
    bits = devices.bit_length() - 1
    rows = -(-(share + D - 1) // D)
    rows = -(-rows // 32) * 32
    far = list(range(bits - 1, 2, -1))
    orders = [far + [1, 2, 0], far + [2, 1, 0]]
    half = rows // 2
    if half % 16 == 0 and half > 16:
        first = -(-half // 2 // 16) * 16
        sizes = [first, first, half - first, half - first]
    else:
        sizes = [half, half]
    parts = []
    start = 0
    for index, size in enumerate(sizes):
        parts.append((start, size, orders[index % 2]))
        start += size
    return bits, rows, parts


def place(device, order):
    spot = 0
    for index, bit in enumerate(order):
        spot = spot + ((device // 2**bit) % 2) * 2**index
    return spot


def other(device, bit):
    step = 2**bit
    return device + step - 2 * step * ((device // step) % 2)


def greet(me, bits):
    barrier = pltpu.get_barrier_semaphore()
    for bit in range(bits):
        pl.semaphore_signal(
            barrier, inc=1, device_id=(other(me, bit),), device_id_type=pl.DeviceIdType.MESH
        )
    pl.semaphore_wait(barrier, bits)


def gather_kernel(devices, share, shard, w_qkv, w_out, w_up, w_down, tail, lines, *rest):
    bits, rows, parts = plan(devices, share)
    slots = rest[: len(parts)]
    local_sem, send_sem, recv_sem = rest[len(parts) :]
    me = lax.axis_index("dp")
    own = []
    for index, (start, size, order) in enumerate(parts):
        copy = pltpu.make_async_copy(
            shard.at[pl.ds(start, size)], slots[index].at[place(me, order)], local_sem.at[index]
        )
        copy.start()
        own.append(copy)
    greet(me, bits)
    for copy in own:
        copy.wait()
    waiting = [None] * len(parts)
    for stage in range(bits):
        for index, (start, size, order) in enumerate(parts):
            if waiting[index] is not None:
                waiting[index].wait()
            block = 2**stage
            begin = (place(me, order) // block) * block
            piece = slots[index].at[pl.ds(begin, block)]
            copy = pltpu.make_async_remote_copy(
                src_ref=piece,
                dst_ref=piece,
                send_sem=send_sem.at[index, stage],
                recv_sem=recv_sem.at[index, stage],
                device_id=(other(me, order[stage]),),
                device_id_type=pl.DeviceIdType.MESH,
            )
            copy.start()
            waiting[index] = copy
    for copy in waiting:
        copy.wait()
    chunks = D // LANES
    for device in range(devices):
        first = device * share // D
        shared = device * share % D != 0
        for index, (start, size, order) in enumerate(parts):
            spot = place(device, order)
            at = first + start
            for chunk in range(chunks):
                if start == 0 and shared:
                    before = lines[chunk, at : at + 1, :]
                lines[chunk, at : at + size, :] = slots[index][
                    spot, :, chunk * LANES : (chunk + 1) * LANES
                ].astype(jnp.float32)
                if start == 0 and shared:
                    lines[chunk, at : at + 1, :] = lines[chunk, at : at + 1, :] + before
    spread(lines, 0, w_qkv, 3)
    spread(lines, 1152, w_out, 1)
    spread(lines, 1536, w_up, 4)
    spread(lines, 3072, w_down, 1)
    spread(lines, 4608, tail, 1)


def spread(lines, first, out, times):
    height = out.shape[0]
    for column in range(times):
        for chunk in range(D // LANES):
            if times == 1:
                value = lines[chunk, first : first + height, :]
            else:
                value = lines[chunk, pl.ds(first + column, height, stride=times), :]
            at = column * D + chunk * LANES
            out[:, at : at + LANES] = value.astype(out.dtype)


def gather_weights(params, devices):
    share = params.shape[0]
    bits, rows, parts = plan(devices, share)
    offset = (lax.axis_index("dp") * share) % D
    flat = jnp.zeros((rows * D,), jnp.float32)
    flat = lax.dynamic_update_slice(flat, params, (offset,))
    shard = flat.reshape(rows, D).astype(jnp.bfloat16)
    vmem = pl.BlockSpec(memory_space=pltpu.VMEM)
    return pl.pallas_call(
        functools.partial(gather_kernel, devices, share),
        out_shape=(
            jax.ShapeDtypeStruct((D, 3 * D), jnp.bfloat16),
            jax.ShapeDtypeStruct((D, D), jnp.bfloat16),
            jax.ShapeDtypeStruct((D, FF), jnp.bfloat16),
            jax.ShapeDtypeStruct((FF, D), jnp.bfloat16),
            jax.ShapeDtypeStruct((16, D), jnp.float32),
        ),
        in_specs=[vmem],
        out_specs=[vmem] * 5,
        scratch_shapes=[pltpu.VMEM((D // LANES, LINES + rows + 24, LANES), jnp.float32)]
        + [pltpu.VMEM((devices, size, D), jnp.bfloat16) for _, size, _ in parts]
        + [
            pltpu.SemaphoreType.DMA((len(parts),)),
            pltpu.SemaphoreType.DMA((len(parts), bits)),
            pltpu.SemaphoreType.DMA((len(parts), bits)),
        ],
        compiler_params=pltpu.CompilerParams(
            collective_id=0, has_side_effects=True, vmem_limit_bytes=60 * 2**20
        ),
    )(shard)


def scatter_kernel(devices, share, g_qkv, g_out, g_up, g_down, g_tail, out, lines, *rest):
    bits, rows, parts = plan(devices, share)
    count = len(parts)
    slots, landed, sums = rest[:count], rest[count : 2 * count], rest[2 * count : 3 * count]
    send_sem, recv_sem = rest[3 * count :]
    me = lax.axis_index("dp")
    collect(lines, 0, g_qkv, 3)
    collect(lines, 1152, g_out, 1)
    collect(lines, 1536, g_up, 4)
    collect(lines, 3072, g_down, 1)
    collect(lines, 4608, g_tail, 1)
    lines[:, 4624:, :] = jnp.zeros_like(lines[:, 4624:, :])
    for device in range(devices):
        first = device * share // D
        for index, (start, size, order) in enumerate(parts):
            spot = place(device, order)
            at = first + start
            for chunk in range(D // LANES):
                slots[index][spot, :, chunk * LANES : (chunk + 1) * LANES] = lines[
                    chunk, at : at + size, :
                ].astype(jnp.bfloat16)
    greet(me, bits)
    waiting = [None] * count

    def send(index, stage):
        order = parts[index][2]
        block = 2**stage
        spot = place(me, order) // block
        away = spot + 1 - 2 * (spot % 2)
        copy = pltpu.make_async_remote_copy(
            src_ref=slots[index].at[pl.ds(away * block, block)],
            dst_ref=landed[index].at[pl.ds(block - 1, block)],
            send_sem=send_sem.at[index, stage],
            recv_sem=recv_sem.at[index, stage],
            device_id=(other(me, order[stage]),),
            device_id_type=pl.DeviceIdType.MESH,
        )
        copy.start()
        return copy

    for index in range(count):
        waiting[index] = send(index, bits - 1)
    for stage in range(bits - 1, -1, -1):
        for index, (start, size, order) in enumerate(parts):
            waiting[index].wait()
            block = 2**stage
            begin = (place(me, order) // block) * block
            if stage == 0:
                piece = sums[index][begin] if bits > 1 else slots[index][begin].astype(jnp.float32)
                out[start : start + size, :] = piece + landed[index][0].astype(jnp.float32)
                continue

            def add(step, carry, index=index, begin=begin, block=block, stage=stage):
                spot = begin + step
                if stage == bits - 1:
                    old = slots[index][spot].astype(jnp.float32)
                else:
                    old = sums[index][spot]
                new = old + landed[index][block - 1 + step].astype(jnp.float32)
                sums[index][spot] = new
                slots[index][spot] = new.astype(jnp.bfloat16)
                return carry

            lax.fori_loop(0, block, add, 0)
            waiting[index] = send(index, stage - 1)


def collect(lines, first, grads, times):
    height = grads.shape[0]
    for column in range(times):
        for chunk in range(D // LANES):
            at = column * D + chunk * LANES
            value = grads[:, at : at + LANES]
            if times == 1:
                lines[chunk, first : first + height, :] = value
            else:
                lines[chunk, pl.ds(first + column, height, stride=times), :] = value


def scatter_grads(grads, devices, share):
    bits, rows, parts = plan(devices, share)
    vmem = pl.BlockSpec(memory_space=pltpu.VMEM)
    total = pl.pallas_call(
        functools.partial(scatter_kernel, devices, share),
        out_shape=jax.ShapeDtypeStruct((rows, D), jnp.float32),
        in_specs=[vmem] * 5,
        out_specs=vmem,
        scratch_shapes=[pltpu.VMEM((D // LANES, LINES + rows + 24, LANES), jnp.float32)]
        + [pltpu.VMEM((devices, size, D), jnp.bfloat16) for _, size, _ in parts]
        + [pltpu.VMEM((devices, size, D), jnp.bfloat16) for _, size, _ in parts]
        + [pltpu.VMEM((devices, size, D), jnp.float32) for _, size, _ in parts]
        + [
            pltpu.SemaphoreType.DMA((len(parts), bits)),
            pltpu.SemaphoreType.DMA((len(parts), bits)),
        ],
        compiler_params=pltpu.CompilerParams(
            collective_id=1, has_side_effects=True, vmem_limit_bytes=63 * 2**20
        ),
    )(*grads)
    offset = (lax.axis_index("dp") * share) % D
    return lax.dynamic_slice(total.reshape(-1), (offset,), (share,))


def token_sum(left, right):
    return lax.dot_general(
        left, right, (((0,), (0,)), ((), ())), preferred_element_type=jnp.float32
    )


def times_t(left, right):
    return lax.dot_general(
        left, right, (((1,), (1,)), ((), ())), preferred_element_type=jnp.float32
    )


def layer_norm(values):
    center = values - jnp.mean(values, axis=-1, keepdims=True)
    factor = lax.rsqrt(jnp.mean(center * center, axis=-1, keepdims=True) + 1e-06)
    return (center * factor, factor)


def norm_back(grad_hat, normed, factor):
    return factor * (
        grad_hat
        - jnp.mean(grad_hat, axis=-1, keepdims=True)
        - normed * jnp.mean(grad_hat * normed, axis=-1, keepdims=True)
    )


PAD = -(-SEQ // 16) * 16
DEEP = D // HEADS


def dot(left, right):
    return lax.dot_general(
        left, right, (((1,), (0,)), ((), ())), preferred_element_type=jnp.float32
    )


def column_sum(values):
    return jnp.sum(values, axis=0, keepdims=True)


def block_kernel(
    images,
    tokens,
    cotangent,
    w_qkv,
    w_out,
    w_up,
    w_down,
    tail,
    result,
    grad_tokens,
    g_qkv,
    g_out,
    g_up,
    g_down,
    g_tail,
    x,
    dy,
    xhat,
    mid,
    a16,
    c16,
    q16,
    k16,
    v16,
    o16,
    probs,
    wide,
    slope,
    act16,
    du16,
    dh,
    do16,
    dqkv,
    dqkv16,
):
    rows = images * PAD
    bf16 = jnp.bfloat16
    for image in range(images):
        for here, there in ((x, tokens), (dy, cotangent)):
            begin = image * PAD
            last = SEQ // 8 * 8
            here[begin + last : begin + PAD, :] = jnp.zeros((PAD - last, D), jnp.float32)
            here[begin : begin + SEQ, :] = there[image]
    normed, factor_in = layer_norm(x[...])
    xhat[...] = normed
    a16[...] = (normed * tail[0:1, :] + tail[1:2, :]).astype(bf16)
    q16[...] = (dot(a16[...], w_qkv[:, 0:D]) + tail[2:3, :]).astype(bf16)
    k16[...] = dot(a16[...], w_qkv[:, D : 2 * D]).astype(bf16)
    v16[...] = (dot(a16[...], w_qkv[:, 2 * D :]) + tail[3:4, :]).astype(bf16)
    scale = DEEP ** (-0.5)
    inside = lax.broadcasted_iota(jnp.int32, (PAD, PAD), 1) < SEQ

    def attend(image, carry):
        span = pl.ds(pl.multiple_of(image * PAD, 16), PAD)
        for head in range(HEADS):
            at = slice(head * DEEP, (head + 1) * DEEP)
            scores = times_t(q16[span, at], k16[span, at]) * scale
            scores = jnp.where(inside, scores, -1e30)
            raw = jnp.exp(scores - jnp.max(scores, axis=-1, keepdims=True))
            full = raw / jnp.sum(raw, axis=-1, keepdims=True)
            probs[image, head] = full
            o16[span, at] = dot(full.astype(bf16), v16[span, at]).astype(bf16)
        return carry

    lax.fori_loop(0, images, attend, 0)
    hidden = x[...] + (dot(o16[...], w_out[...]) + tail[4:5, :])
    x[...] = hidden
    normed, factor_mid = layer_norm(hidden)
    mid[...] = normed
    c16[...] = (normed * tail[5:6, :] + tail[6:7, :]).astype(bf16)
    for column in range(FF // D):
        at = slice(column * D, (column + 1) * D)
        wide[:, at] = dot(c16[...], w_up[:, at]) + tail[8 + column : 9 + column, :]
    step = 16

    def gelu(index, carry):
        span = pl.ds(pl.multiple_of(index * step, step), step)
        pre = wide[span, :]
        phi = 0.5 * (1.0 + lax.erf(pre * 0.7071067811865476))
        act16[span, :] = (pre * phi).astype(bf16)
        slope[span, :] = phi + pre * jnp.exp(-0.5 * pre * pre) * 0.3989422804014327
        return carry

    lax.fori_loop(0, rows // step, gelu, 0)
    final = x[...] + (dot(act16[...], w_down[...]) + tail[7:8, :])
    for image in range(images):
        result[image] = final[image * PAD : image * PAD + SEQ, :]

    dy16 = dy[...].astype(bf16)
    g_down[...] = token_sum(act16[...], dy16)
    g_tail[7:8, :] = column_sum(dy[...])
    wide[...] = times_t(dy16, w_down[...])

    def grad_pre(index, total):
        span = pl.ds(pl.multiple_of(index * step, step), step)
        value = wide[span, :] * slope[span, :]
        du16[span, :] = value.astype(bf16)
        return total + value

    total = lax.fori_loop(0, rows // step, grad_pre, jnp.zeros((step, FF), jnp.float32))
    total = column_sum(total)
    for column in range(FF // D):
        g_tail[8 + column : 9 + column, :] = total[:, column * D : (column + 1) * D]
    g_tail[12:16, :] = jnp.zeros((4, D), jnp.float32)
    g_up[...] = token_sum(c16[...], du16[...])
    grad_mlp = times_t(du16[...], w_up[...])
    g_tail[5:6, :] = column_sum(grad_mlp * mid[...])
    g_tail[6:7, :] = column_sum(grad_mlp)
    grad_hidden = dy[...] + norm_back(grad_mlp * tail[5:6, :], mid[...], factor_mid)
    dh[...] = grad_hidden
    g_tail[4:5, :] = column_sum(grad_hidden)
    dh16 = grad_hidden.astype(bf16)
    g_out[...] = token_sum(o16[...], dh16)
    do16[...] = times_t(dh16, w_out[...]).astype(bf16)

    def attend_back(image, carry):
        span = pl.ds(pl.multiple_of(image * PAD, 16), PAD)
        for head in range(HEADS):
            at = slice(head * DEEP, (head + 1) * DEEP)
            full = probs[image, head]
            grad_o = do16[span, at]
            dqkv[span, 2 * D + head * DEEP : 2 * D + (head + 1) * DEEP] = token_sum(
                full.astype(bf16), grad_o
            )
            grad_probs = times_t(grad_o, v16[span, at])
            delta = jnp.sum(full * grad_probs, axis=-1, keepdims=True)
            grad_scores = (full * (grad_probs - delta) * scale).astype(bf16)
            dqkv[span, at] = dot(grad_scores, k16[span, at])
            dqkv[span, D + head * DEEP : D + (head + 1) * DEEP] = token_sum(
                grad_scores, q16[span, at]
            )
        return carry

    lax.fori_loop(0, images, attend_back, 0)
    g_tail[2:3, :] = column_sum(dqkv[:, 0:D])
    g_tail[3:4, :] = column_sum(dqkv[:, 2 * D :])
    dqkv16[...] = dqkv[...].astype(bf16)
    g_qkv[...] = token_sum(a16[...], dqkv16[...])
    grad_in = times_t(dqkv16[...], w_qkv[...])
    g_tail[0:1, :] = column_sum(grad_in * xhat[...])
    g_tail[1:2, :] = column_sum(grad_in)
    final = dh[...] + norm_back(grad_in * tail[0:1, :], xhat[...], factor_in)
    for image in range(images):
        grad_tokens[image] = final[image * PAD : image * PAD + SEQ, :]


def block_scratch(images):
    rows = images * PAD
    f32, bf16 = jnp.float32, jnp.bfloat16
    return [
        pltpu.VMEM(shape, kind)
        for shape, kind in (
            ((rows, D), f32),
            ((rows, D), f32),
            ((rows, D), f32),
            ((rows, D), f32),
            ((rows, D), bf16),
            ((rows, D), bf16),
            ((rows, D), bf16),
            ((rows, D), bf16),
            ((rows, D), bf16),
            ((rows, D), bf16),
            ((images, HEADS, PAD, PAD), f32),
            ((rows, FF), f32),
            ((rows, FF), f32),
            ((rows, FF), bf16),
            ((rows, FF), bf16),
            ((rows, D), f32),
            ((rows, D), bf16),
            ((rows, 3 * D), f32),
            ((rows, 3 * D), bf16),
        )
    ]


def block(tokens, cotangent, weights):
    images = tokens.shape[0]
    f32 = jnp.float32
    vmem = pl.BlockSpec(memory_space=pltpu.VMEM)
    return pl.pallas_call(
        functools.partial(block_kernel, images),
        out_shape=tuple(
            jax.ShapeDtypeStruct(shape, f32)
            for shape in (
                tokens.shape,
                tokens.shape,
                (D, 3 * D),
                (D, D),
                (D, FF),
                (FF, D),
                (16, D),
            )
        ),
        in_specs=[vmem] * 7,
        out_specs=[vmem] * 7,
        scratch_shapes=block_scratch(images),
        compiler_params=pltpu.CompilerParams(vmem_limit_bytes=63 * 2**20),
    )(tokens, cotangent, *weights)


def adamw(params, grads, first, second, position):
    first_end = 3 * D * D
    second_end = first_end + D * D
    third_end = second_end + D * FF
    fourth_end = third_end + FF * D
    rate = jnp.where(
        position < first_end,
        0.01,
        jnp.where(
            position < second_end,
            0.1,
            jnp.where(position < third_end, 0.01, jnp.where(position < fourth_end, 0.005, 0.1)),
        ),
    )
    first_new = 0.9 * first + 0.1 * grads
    second_new = 0.999 * second + 0.001 * grads * grads
    update = (
        first_new / (1.0 - 0.9**STEP) / (jnp.sqrt(second_new / (1.0 - 0.999**STEP)) + 1e-08)
        + 0.1 * params
    )
    return (params - rate * update, first_new, second_new)


def per_device(tokens, params, moment1, moment2, cotangent):
    devices = lax.axis_size("dp")
    length = params.shape[0]
    weights = gather_weights(params, devices)
    result, grad_tokens, *grads = block(tokens, cotangent, weights)
    shares = scatter_grads(grads, devices, length)
    count = tokens.shape[0] * tokens.shape[1] * devices
    grad_params = shares * (1.0 / math.sqrt(count))
    position = lax.axis_index("dp") * length + jnp.arange(length, dtype=jnp.int32)
    new_params, new_first, new_second = adamw(params, grad_params, moment1, moment2, position)
    return (result, grad_tokens, grad_params, new_params, new_first, new_second)


def solution(mesh):
    in_specs = (P("dp", None, None), P("dp"), P("dp"), P("dp"), P("dp", None, None))
    out_specs = (P("dp", None, None), P("dp", None, None), P("dp"), P("dp"), P("dp"), P("dp"))
    return jax.shard_map(
        per_device, mesh=mesh, in_specs=in_specs, out_specs=out_specs, check_vma=False
    )
```

```python
import math

import jax
import jax.numpy as jnp
from jax import lax
from jax.experimental import pallas as pl
from jax.experimental.pallas import tpu as pltpu
import functools
from jax.sharding import PartitionSpec as P

D = 384
HEADS = 6
FF = 1536
SEQ = 197
STEP = 3


LANES = 128
LINES = 4 * 1152 + 12


def plan(devices, share, late=False):
    bits = devices.bit_length() - 1
    rows = -(-(share + D - 1) // D)
    rows = -(-rows // 32) * 32
    far = list(range(bits - 1, 2, -1))
    orders = [far + [1, 2, 0], far + [2, 1, 0]]
    units = rows // 32
    waves = min(3, units)
    sizes = [16 * (units * (wave + 1) // waves - units * wave // waves) for wave in range(waves)]
    sizes.sort(reverse=late)
    parts = []
    start = 0
    for size in sizes:
        for order in orders:
            parts.append((start, size, order))
            start += size
    return bits, rows, parts


def place(device, order):
    spot = 0
    for index, bit in enumerate(order):
        spot = spot + ((device // 2**bit) % 2) * 2**index
    return spot


def other(device, bit):
    step = 2**bit
    return device + step - 2 * step * ((device // step) % 2)


def greet(me, bits):
    barrier = pltpu.get_barrier_semaphore()
    for bit in range(bits):
        pl.semaphore_signal(
            barrier, inc=1, device_id=(other(me, bit),), device_id_type=pl.DeviceIdType.MESH
        )
    pl.semaphore_wait(barrier, bits)


def gather_kernel(devices, share, shard, w_qkv, w_out, w_up, w_down, tail, lines, *rest):
    bits, rows, parts = plan(devices, share)
    slots = rest[: len(parts)]
    local_sem, send_sem, recv_sem = rest[len(parts) :]
    me = lax.axis_index("dp")
    own = []
    for index, (start, size, order) in enumerate(parts):
        copy = pltpu.make_async_copy(
            shard.at[pl.ds(start, size)], slots[index].at[place(me, order)], local_sem.at[index]
        )
        copy.start()
        own.append(copy)
    greet(me, bits)
    for copy in own:
        copy.wait()
    waiting = [None] * len(parts)
    pairs = len(parts) // 2
    for wave in range(bits + pairs - 1):
        for index, (start, size, order) in enumerate(parts):
            stage = wave - index // 2
            if not 0 <= stage < bits:
                continue
            if waiting[index] is not None:
                waiting[index].wait()
            block = 2**stage
            begin = (place(me, order) // block) * block
            piece = slots[index].at[pl.ds(begin, block)]
            copy = pltpu.make_async_remote_copy(
                src_ref=piece,
                dst_ref=piece,
                send_sem=send_sem.at[index, stage],
                recv_sem=recv_sem.at[index, stage],
                device_id=(other(me, order[stage]),),
                device_id_type=pl.DeviceIdType.MESH,
            )
            copy.start()
            waiting[index] = copy
    for copy in waiting:
        copy.wait()
    chunks = D // LANES
    for device in range(devices):
        first = device * share // D
        shared = device * share % D != 0
        for index, (start, size, order) in enumerate(parts):
            spot = place(device, order)
            at = first + start
            for chunk in range(chunks):
                if start == 0 and shared:
                    before = lines[chunk, at : at + 1, :]
                lines[chunk, at : at + size, :] = slots[index][
                    spot, :, chunk * LANES : (chunk + 1) * LANES
                ].astype(jnp.float32)
                if start == 0 and shared:
                    lines[chunk, at : at + 1, :] = lines[chunk, at : at + 1, :] + before
    spread(lines, 0, w_qkv, 3)
    spread(lines, 1152, w_out, 1)
    spread(lines, 1536, w_up, 4)
    spread(lines, 3072, w_down, 1)
    spread(lines, 4608, tail, 1)


def spread(lines, first, out, times):
    height = out.shape[0]
    for column in range(times):
        for chunk in range(D // LANES):
            if times == 1:
                value = lines[chunk, first : first + height, :]
            else:
                value = lines[chunk, pl.ds(first + column, height, stride=times), :]
            at = column * D + chunk * LANES
            out[:, at : at + LANES] = value.astype(out.dtype)


def gather_weights(params, devices):
    share = params.shape[0]
    bits, rows, parts = plan(devices, share)
    offset = (lax.axis_index("dp") * share) % D
    flat = jnp.zeros((rows * D,), jnp.float32)
    flat = lax.dynamic_update_slice(flat, params, (offset,))
    shard = flat.reshape(rows, D).astype(jnp.bfloat16)
    vmem = pl.BlockSpec(memory_space=pltpu.VMEM)
    return pl.pallas_call(
        functools.partial(gather_kernel, devices, share),
        out_shape=(
            jax.ShapeDtypeStruct((D, 3 * D), jnp.bfloat16),
            jax.ShapeDtypeStruct((D, D), jnp.bfloat16),
            jax.ShapeDtypeStruct((D, FF), jnp.bfloat16),
            jax.ShapeDtypeStruct((FF, D), jnp.bfloat16),
            jax.ShapeDtypeStruct((16, D), jnp.float32),
        ),
        in_specs=[vmem],
        out_specs=[vmem] * 5,
        scratch_shapes=[pltpu.VMEM((D // LANES, LINES + rows + 24, LANES), jnp.float32)]
        + [pltpu.VMEM((devices, size, D), jnp.bfloat16) for _, size, _ in parts]
        + [
            pltpu.SemaphoreType.DMA((len(parts),)),
            pltpu.SemaphoreType.DMA((len(parts), bits)),
            pltpu.SemaphoreType.DMA((len(parts), bits)),
        ],
        compiler_params=pltpu.CompilerParams(
            collective_id=0, has_side_effects=True, vmem_limit_bytes=60 * 2**20
        ),
    )(shard)


def scatter_kernel(devices, share, g_qkv, g_out, g_up, g_down, g_tail, out, lines, *rest):
    bits, rows, parts = plan(devices, share, True)
    count = len(parts)
    slots, landed, sums = rest[:count], rest[count : 2 * count], rest[2 * count : 3 * count]
    send_sem, recv_sem = rest[3 * count :]
    me = lax.axis_index("dp")
    collect(lines, 0, g_qkv, 3)
    collect(lines, 1152, g_out, 1)
    collect(lines, 1536, g_up, 4)
    collect(lines, 3072, g_down, 1)
    collect(lines, 4608, g_tail, 1)
    lines[:, 4624:, :] = jnp.zeros_like(lines[:, 4624:, :])

    def pack(index):
        start, size, order = parts[index]
        for device in range(devices):
            spot = place(device, order)
            at = device * share // D + start
            for chunk in range(D // LANES):
                slots[index][spot, :, chunk * LANES : (chunk + 1) * LANES] = lines[
                    chunk, at : at + size, :
                ].astype(jnp.bfloat16)

    greet(me, bits)
    waiting = [None] * count

    def send(index, stage):
        order = parts[index][2]
        block = 2**stage
        spot = place(me, order) // block
        away = spot + 1 - 2 * (spot % 2)
        copy = pltpu.make_async_remote_copy(
            src_ref=slots[index].at[pl.ds(away * block, block)],
            dst_ref=landed[index].at[pl.ds(block - 1, block)],
            send_sem=send_sem.at[index, stage],
            recv_sem=recv_sem.at[index, stage],
            device_id=(other(me, order[stage]),),
            device_id_type=pl.DeviceIdType.MESH,
        )
        copy.start()
        return copy

    for wave in range(bits + count // 2):
        for index, (start, size, order) in enumerate(parts):
            stage = bits - wave + index // 2
            if not 0 <= stage <= bits:
                continue
            if stage == bits:
                pack(index)
                waiting[index] = send(index, bits - 1)
                continue
            waiting[index].wait()
            block = 2**stage
            begin = (place(me, order) // block) * block
            if stage == 0:
                piece = sums[index][begin] if bits > 1 else slots[index][begin].astype(jnp.float32)
                out[start : start + size, :] = piece + landed[index][0].astype(jnp.float32)
                continue

            def add(step, carry, index=index, begin=begin, block=block, stage=stage):
                spot = begin + step
                if stage == bits - 1:
                    old = slots[index][spot].astype(jnp.float32)
                else:
                    old = sums[index][spot]
                new = old + landed[index][block - 1 + step].astype(jnp.float32)
                sums[index][spot] = new
                slots[index][spot] = new.astype(jnp.bfloat16)
                return carry

            lax.fori_loop(0, block, add, 0)
            waiting[index] = send(index, stage - 1)


def collect(lines, first, grads, times):
    height = grads.shape[0]
    for column in range(times):
        for chunk in range(D // LANES):
            at = column * D + chunk * LANES
            value = grads[:, at : at + LANES]
            if times == 1:
                lines[chunk, first : first + height, :] = value
            else:
                lines[chunk, pl.ds(first + column, height, stride=times), :] = value


def scatter_grads(grads, devices, share):
    bits, rows, parts = plan(devices, share, True)
    vmem = pl.BlockSpec(memory_space=pltpu.VMEM)
    total = pl.pallas_call(
        functools.partial(scatter_kernel, devices, share),
        out_shape=jax.ShapeDtypeStruct((rows, D), jnp.float32),
        in_specs=[vmem] * 5,
        out_specs=vmem,
        scratch_shapes=[pltpu.VMEM((D // LANES, LINES + rows + 24, LANES), jnp.float32)]
        + [pltpu.VMEM((devices, size, D), jnp.bfloat16) for _, size, _ in parts]
        + [pltpu.VMEM((devices, size, D), jnp.bfloat16) for _, size, _ in parts]
        + [pltpu.VMEM((devices, size, D), jnp.float32) for _, size, _ in parts]
        + [
            pltpu.SemaphoreType.DMA((len(parts), bits)),
            pltpu.SemaphoreType.DMA((len(parts), bits)),
        ],
        compiler_params=pltpu.CompilerParams(
            collective_id=1, has_side_effects=True, vmem_limit_bytes=63 * 2**20
        ),
    )(*grads)
    offset = (lax.axis_index("dp") * share) % D
    return lax.dynamic_slice(total.reshape(-1), (offset,), (share,))


def token_sum(left, right):
    return lax.dot_general(
        left, right, (((0,), (0,)), ((), ())), preferred_element_type=jnp.float32
    )


def times_t(left, right):
    return lax.dot_general(
        left, right, (((1,), (1,)), ((), ())), preferred_element_type=jnp.float32
    )


def layer_norm(values):
    center = values - jnp.mean(values, axis=-1, keepdims=True)
    factor = lax.rsqrt(jnp.mean(center * center, axis=-1, keepdims=True) + 1e-06)
    return (center * factor, factor)


def norm_back(grad_hat, normed, factor):
    return factor * (
        grad_hat
        - jnp.mean(grad_hat, axis=-1, keepdims=True)
        - normed * jnp.mean(grad_hat * normed, axis=-1, keepdims=True)
    )


PAD = -(-SEQ // 16) * 16
DEEP = D // HEADS


def dot(left, right):
    return lax.dot_general(
        left, right, (((1,), (0,)), ((), ())), preferred_element_type=jnp.float32
    )


def column_sum(values):
    return jnp.sum(values, axis=0, keepdims=True)


def block_kernel(
    images,
    tokens,
    cotangent,
    w_qkv,
    w_out,
    w_up,
    w_down,
    tail,
    result,
    grad_tokens,
    g_qkv,
    g_out,
    g_up,
    g_down,
    g_tail,
    x,
    dy,
    xhat,
    mid,
    a16,
    c16,
    q16,
    k16,
    v16,
    o16,
    probs,
    wide,
    slope,
    act16,
    du16,
    dh,
    do16,
    dqkv,
    dqkv16,
):
    rows = images * PAD
    bf16 = jnp.bfloat16
    for image in range(images):
        for here, there in ((x, tokens), (dy, cotangent)):
            begin = image * PAD
            last = SEQ // 8 * 8
            here[begin + last : begin + PAD, :] = jnp.zeros((PAD - last, D), jnp.float32)
            here[begin : begin + SEQ, :] = there[image]
    normed, factor_in = layer_norm(x[...])
    xhat[...] = normed
    a16[...] = (normed * tail[0:1, :] + tail[1:2, :]).astype(bf16)
    q16[...] = (dot(a16[...], w_qkv[:, 0:D]) + tail[2:3, :]).astype(bf16)
    k16[...] = dot(a16[...], w_qkv[:, D : 2 * D]).astype(bf16)
    v16[...] = (dot(a16[...], w_qkv[:, 2 * D :]) + tail[3:4, :]).astype(bf16)
    scale = DEEP ** (-0.5)
    inside = lax.broadcasted_iota(jnp.int32, (PAD, PAD), 1) < SEQ

    def attend(image, carry):
        span = pl.ds(pl.multiple_of(image * PAD, 16), PAD)
        for head in range(HEADS):
            at = slice(head * DEEP, (head + 1) * DEEP)
            scores = times_t(q16[span, at], k16[span, at]) * scale
            scores = jnp.where(inside, scores, -1e30)
            raw = jnp.exp(scores - jnp.max(scores, axis=-1, keepdims=True))
            full = raw / jnp.sum(raw, axis=-1, keepdims=True)
            probs[image, head] = full
            o16[span, at] = dot(full.astype(bf16), v16[span, at]).astype(bf16)
        return carry

    lax.fori_loop(0, images, attend, 0)
    hidden = x[...] + (dot(o16[...], w_out[...]) + tail[4:5, :])
    x[...] = hidden
    normed, factor_mid = layer_norm(hidden)
    mid[...] = normed
    c16[...] = (normed * tail[5:6, :] + tail[6:7, :]).astype(bf16)
    for column in range(FF // D):
        at = slice(column * D, (column + 1) * D)
        wide[:, at] = dot(c16[...], w_up[:, at]) + tail[8 + column : 9 + column, :]
    step = 16

    def gelu(index, carry):
        span = pl.ds(pl.multiple_of(index * step, step), step)
        pre = wide[span, :]
        phi = 0.5 * (1.0 + lax.erf(pre * 0.7071067811865476))
        act16[span, :] = (pre * phi).astype(bf16)
        slope[span, :] = phi + pre * jnp.exp(-0.5 * pre * pre) * 0.3989422804014327
        return carry

    lax.fori_loop(0, rows // step, gelu, 0)
    final = x[...] + (dot(act16[...], w_down[...]) + tail[7:8, :])
    for image in range(images):
        result[image] = final[image * PAD : image * PAD + SEQ, :]

    dy16 = dy[...].astype(bf16)
    g_down[...] = token_sum(act16[...], dy16)
    g_tail[7:8, :] = column_sum(dy[...])
    wide[...] = times_t(dy16, w_down[...])

    def grad_pre(index, total):
        span = pl.ds(pl.multiple_of(index * step, step), step)
        value = wide[span, :] * slope[span, :]
        du16[span, :] = value.astype(bf16)
        return total + value

    total = lax.fori_loop(0, rows // step, grad_pre, jnp.zeros((step, FF), jnp.float32))
    total = column_sum(total)
    for column in range(FF // D):
        g_tail[8 + column : 9 + column, :] = total[:, column * D : (column + 1) * D]
    g_tail[12:16, :] = jnp.zeros((4, D), jnp.float32)
    g_up[...] = token_sum(c16[...], du16[...])
    grad_mlp = times_t(du16[...], w_up[...])
    g_tail[5:6, :] = column_sum(grad_mlp * mid[...])
    g_tail[6:7, :] = column_sum(grad_mlp)
    grad_hidden = dy[...] + norm_back(grad_mlp * tail[5:6, :], mid[...], factor_mid)
    dh[...] = grad_hidden
    g_tail[4:5, :] = column_sum(grad_hidden)
    dh16 = grad_hidden.astype(bf16)
    g_out[...] = token_sum(o16[...], dh16)
    do16[...] = times_t(dh16, w_out[...]).astype(bf16)

    def attend_back(image, carry):
        span = pl.ds(pl.multiple_of(image * PAD, 16), PAD)
        for head in range(HEADS):
            at = slice(head * DEEP, (head + 1) * DEEP)
            full = probs[image, head]
            grad_o = do16[span, at]
            dqkv[span, 2 * D + head * DEEP : 2 * D + (head + 1) * DEEP] = token_sum(
                full.astype(bf16), grad_o
            )
            grad_probs = times_t(grad_o, v16[span, at])
            delta = jnp.sum(full * grad_probs, axis=-1, keepdims=True)
            grad_scores = (full * (grad_probs - delta) * scale).astype(bf16)
            dqkv[span, at] = dot(grad_scores, k16[span, at])
            dqkv[span, D + head * DEEP : D + (head + 1) * DEEP] = token_sum(
                grad_scores, q16[span, at]
            )
        return carry

    lax.fori_loop(0, images, attend_back, 0)
    g_tail[2:3, :] = column_sum(dqkv[:, 0:D])
    g_tail[3:4, :] = column_sum(dqkv[:, 2 * D :])
    dqkv16[...] = dqkv[...].astype(bf16)
    g_qkv[...] = token_sum(a16[...], dqkv16[...])
    grad_in = times_t(dqkv16[...], w_qkv[...])
    g_tail[0:1, :] = column_sum(grad_in * xhat[...])
    g_tail[1:2, :] = column_sum(grad_in)
    final = dh[...] + norm_back(grad_in * tail[0:1, :], xhat[...], factor_in)
    for image in range(images):
        grad_tokens[image] = final[image * PAD : image * PAD + SEQ, :]


def block_scratch(images):
    rows = images * PAD
    f32, bf16 = jnp.float32, jnp.bfloat16
    return [
        pltpu.VMEM(shape, kind)
        for shape, kind in (
            ((rows, D), f32),
            ((rows, D), f32),
            ((rows, D), f32),
            ((rows, D), f32),
            ((rows, D), bf16),
            ((rows, D), bf16),
            ((rows, D), bf16),
            ((rows, D), bf16),
            ((rows, D), bf16),
            ((rows, D), bf16),
            ((images, HEADS, PAD, PAD), f32),
            ((rows, FF), f32),
            ((rows, FF), f32),
            ((rows, FF), bf16),
            ((rows, FF), bf16),
            ((rows, D), f32),
            ((rows, D), bf16),
            ((rows, 3 * D), f32),
            ((rows, 3 * D), bf16),
        )
    ]


def block(tokens, cotangent, weights):
    images = tokens.shape[0]
    f32 = jnp.float32
    vmem = pl.BlockSpec(memory_space=pltpu.VMEM)
    return pl.pallas_call(
        functools.partial(block_kernel, images),
        out_shape=tuple(
            jax.ShapeDtypeStruct(shape, f32)
            for shape in (
                tokens.shape,
                tokens.shape,
                (D, 3 * D),
                (D, D),
                (D, FF),
                (FF, D),
                (16, D),
            )
        ),
        in_specs=[vmem] * 7,
        out_specs=[vmem] * 7,
        scratch_shapes=block_scratch(images),
        compiler_params=pltpu.CompilerParams(vmem_limit_bytes=63 * 2**20),
    )(tokens, cotangent, *weights)


def adamw(params, grads, first, second, position):
    first_end = 3 * D * D
    second_end = first_end + D * D
    third_end = second_end + D * FF
    fourth_end = third_end + FF * D
    rate = jnp.where(
        position < first_end,
        0.01,
        jnp.where(
            position < second_end,
            0.1,
            jnp.where(position < third_end, 0.01, jnp.where(position < fourth_end, 0.005, 0.1)),
        ),
    )
    first_new = 0.9 * first + 0.1 * grads
    second_new = 0.999 * second + 0.001 * grads * grads
    update = (
        first_new / (1.0 - 0.9**STEP) / (jnp.sqrt(second_new / (1.0 - 0.999**STEP)) + 1e-08)
        + 0.1 * params
    )
    return (params - rate * update, first_new, second_new)


def per_device(tokens, params, moment1, moment2, cotangent):
    devices = lax.axis_size("dp")
    length = params.shape[0]
    weights = gather_weights(params, devices)
    result, grad_tokens, *grads = block(tokens, cotangent, weights)
    shares = scatter_grads(grads, devices, length)
    count = tokens.shape[0] * tokens.shape[1] * devices
    grad_params = shares * (1.0 / math.sqrt(count))
    position = lax.axis_index("dp") * length + jnp.arange(length, dtype=jnp.int32)
    new_params, new_first, new_second = adamw(params, grad_params, moment1, moment2, position)
    return (result, grad_tokens, grad_params, new_params, new_first, new_second)


def solution(mesh):
    in_specs = (P("dp", None, None), P("dp"), P("dp"), P("dp"), P("dp", None, None))
    out_specs = (P("dp", None, None), P("dp", None, None), P("dp"), P("dp"), P("dp"), P("dp"))
    return jax.shard_map(
        per_device, mesh=mesh, in_specs=in_specs, out_specs=out_specs, check_vma=False
    )
```

```python
import math

import jax
import jax.numpy as jnp
from jax import lax
from jax.experimental import pallas as pl
from jax.experimental.pallas import tpu as pltpu
import functools
from jax.sharding import PartitionSpec as P

D = 384
HEADS = 6
FF = 1536
SEQ = 197
STEP = 3


LANES = 128
LINES = 4 * 1152 + 12


def plan(devices, share):
    bits = devices.bit_length() - 1
    rows = -(-(share + D - 1) // D)
    rows = -(-rows // 32) * 32
    far = list(range(bits - 1, 2, -1))
    orders = [far + [1, 2, 0], far + [2, 1, 0]]
    half = rows // 2
    if half % 16 == 0 and half > 16:
        first = -(-half // 2 // 16) * 16
        sizes = [first, first, half - first, half - first]
    else:
        sizes = [half, half]
    parts = []
    start = 0
    for index, size in enumerate(sizes):
        parts.append((start, size, orders[index % 2]))
        start += size
    return bits, rows, parts


def place(device, order):
    spot = 0
    for index, bit in enumerate(order):
        spot = spot + ((device // 2**bit) % 2) * 2**index
    return spot


def other(device, bit):
    step = 2**bit
    return device + step - 2 * step * ((device // step) % 2)


def greet(me, bits):
    barrier = pltpu.get_barrier_semaphore()
    for bit in range(bits):
        pl.semaphore_signal(
            barrier, inc=1, device_id=(other(me, bit),), device_id_type=pl.DeviceIdType.MESH
        )
    pl.semaphore_wait(barrier, bits)


def gather_kernel(devices, share, shard, w_qkv, w_out, w_up, w_down, tail, lines, *rest):
    bits, rows, parts = plan(devices, share)
    slots = rest[: len(parts)]
    local_sem, send_sem, recv_sem = rest[len(parts) :]
    me = lax.axis_index("dp")
    own = []
    for index, (start, size, order) in enumerate(parts):
        copy = pltpu.make_async_copy(
            shard.at[pl.ds(start, size)], slots[index].at[place(me, order)], local_sem.at[index]
        )
        copy.start()
        own.append(copy)
    greet(me, bits)
    for copy in own:
        copy.wait()
    waiting = [None] * len(parts)
    for stage in range(bits):
        for index, (start, size, order) in enumerate(parts):
            if waiting[index] is not None:
                waiting[index].wait()
            block = 2**stage
            begin = (place(me, order) // block) * block
            piece = slots[index].at[pl.ds(begin, block)]
            copy = pltpu.make_async_remote_copy(
                src_ref=piece,
                dst_ref=piece,
                send_sem=send_sem.at[index, stage],
                recv_sem=recv_sem.at[index, stage],
                device_id=(other(me, order[stage]),),
                device_id_type=pl.DeviceIdType.MESH,
            )
            copy.start()
            waiting[index] = copy
    for copy in waiting:
        copy.wait()
    chunks = D // LANES
    for device in range(devices):
        first = device * share // D
        shared = device * share % D != 0
        for index, (start, size, order) in enumerate(parts):
            spot = place(device, order)
            at = first + start
            for chunk in range(chunks):
                if start == 0 and shared:
                    before = lines[chunk, at : at + 1, :]
                lines[chunk, at : at + size, :] = slots[index][
                    spot, :, chunk * LANES : (chunk + 1) * LANES
                ].astype(jnp.float32)
                if start == 0 and shared:
                    lines[chunk, at : at + 1, :] = lines[chunk, at : at + 1, :] + before
    spread(lines, 0, w_qkv, 3)
    spread(lines, 1152, w_out, 1)
    spread(lines, 1536, w_up, 4)
    spread(lines, 3072, w_down, 1)
    spread(lines, 4608, tail, 1)


def spread(lines, first, out, times):
    height = out.shape[0]
    for column in range(times):
        for chunk in range(D // LANES):
            if times == 1:
                value = lines[chunk, first : first + height, :]
            else:
                value = lines[chunk, pl.ds(first + column, height, stride=times), :]
            at = column * D + chunk * LANES
            out[:, at : at + LANES] = value.astype(out.dtype)


def gather_weights(params, devices):
    share = params.shape[0]
    bits, rows, parts = plan(devices, share)
    offset = (lax.axis_index("dp") * share) % D
    flat = jnp.zeros((rows * D,), jnp.float32)
    flat = lax.dynamic_update_slice(flat, params, (offset,))
    shard = flat.reshape(rows, D).astype(jnp.bfloat16)
    vmem = pl.BlockSpec(memory_space=pltpu.VMEM)
    return pl.pallas_call(
        functools.partial(gather_kernel, devices, share),
        out_shape=(
            jax.ShapeDtypeStruct((D, 3 * D), jnp.bfloat16),
            jax.ShapeDtypeStruct((D, D), jnp.bfloat16),
            jax.ShapeDtypeStruct((D, FF), jnp.bfloat16),
            jax.ShapeDtypeStruct((FF, D), jnp.bfloat16),
            jax.ShapeDtypeStruct((16, D), jnp.float32),
        ),
        in_specs=[vmem],
        out_specs=[vmem] * 5,
        scratch_shapes=[pltpu.VMEM((D // LANES, LINES + rows + 24, LANES), jnp.float32)]
        + [pltpu.VMEM((devices, size, D), jnp.bfloat16) for _, size, _ in parts]
        + [
            pltpu.SemaphoreType.DMA((len(parts),)),
            pltpu.SemaphoreType.DMA((len(parts), bits)),
            pltpu.SemaphoreType.DMA((len(parts), bits)),
        ],
        compiler_params=pltpu.CompilerParams(
            collective_id=0, has_side_effects=True, vmem_limit_bytes=60 * 2**20
        ),
    )(shard)


def scatter_kernel(devices, share, g_qkv, g_out, g_up, g_down, g_tail, out, lines, *rest):
    bits, rows, parts = plan(devices, share)
    count = len(parts)
    slots, landed, sums = rest[:count], rest[count : 2 * count], rest[2 * count : 3 * count]
    send_sem, recv_sem = rest[3 * count :]
    me = lax.axis_index("dp")
    collect(lines, 0, g_qkv, 3)
    collect(lines, 1152, g_out, 1)
    collect(lines, 1536, g_up, 4)
    collect(lines, 3072, g_down, 1)
    collect(lines, 4608, g_tail, 1)
    lines[:, 4624:, :] = jnp.zeros_like(lines[:, 4624:, :])

    def pack(index):
        start, size, order = parts[index]
        for device in range(devices):
            spot = place(device, order)
            at = device * share // D + start
            for chunk in range(D // LANES):
                slots[index][spot, :, chunk * LANES : (chunk + 1) * LANES] = lines[
                    chunk, at : at + size, :
                ].astype(jnp.bfloat16)

    greet(me, bits)
    waiting = [None] * count

    def send(index, stage):
        order = parts[index][2]
        block = 2**stage
        spot = place(me, order) // block
        away = spot + 1 - 2 * (spot % 2)
        copy = pltpu.make_async_remote_copy(
            src_ref=slots[index].at[pl.ds(away * block, block)],
            dst_ref=landed[index].at[pl.ds(block - 1, block)],
            send_sem=send_sem.at[index, stage],
            recv_sem=recv_sem.at[index, stage],
            device_id=(other(me, order[stage]),),
            device_id_type=pl.DeviceIdType.MESH,
        )
        copy.start()
        return copy

    for index in range(count):
        pack(index)
        waiting[index] = send(index, bits - 1)
    for stage in range(bits - 1, -1, -1):
        for index, (start, size, order) in enumerate(parts):
            waiting[index].wait()
            block = 2**stage
            begin = (place(me, order) // block) * block
            if stage == 0:
                piece = sums[index][begin] if bits > 1 else slots[index][begin].astype(jnp.float32)
                out[start : start + size, :] = piece + landed[index][0].astype(jnp.float32)
                continue

            def add(step, carry, index=index, begin=begin, block=block, stage=stage):
                spot = begin + step
                if stage == bits - 1:
                    old = slots[index][spot].astype(jnp.float32)
                else:
                    old = sums[index][spot]
                new = old + landed[index][block - 1 + step].astype(jnp.float32)
                sums[index][spot] = new
                slots[index][spot] = new.astype(jnp.bfloat16)
                return carry

            lax.fori_loop(0, block, add, 0)
            waiting[index] = send(index, stage - 1)


def collect(lines, first, grads, times):
    height = grads.shape[0]
    for column in range(times):
        for chunk in range(D // LANES):
            at = column * D + chunk * LANES
            value = grads[:, at : at + LANES]
            if times == 1:
                lines[chunk, first : first + height, :] = value
            else:
                lines[chunk, pl.ds(first + column, height, stride=times), :] = value


def scatter_grads(grads, devices, share):
    bits, rows, parts = plan(devices, share)
    vmem = pl.BlockSpec(memory_space=pltpu.VMEM)
    total = pl.pallas_call(
        functools.partial(scatter_kernel, devices, share),
        out_shape=jax.ShapeDtypeStruct((rows, D), jnp.float32),
        in_specs=[vmem] * 5,
        out_specs=vmem,
        scratch_shapes=[pltpu.VMEM((D // LANES, LINES + rows + 24, LANES), jnp.float32)]
        + [pltpu.VMEM((devices, size, D), jnp.bfloat16) for _, size, _ in parts]
        + [pltpu.VMEM((devices, size, D), jnp.bfloat16) for _, size, _ in parts]
        + [pltpu.VMEM((devices, size, D), jnp.float32) for _, size, _ in parts]
        + [
            pltpu.SemaphoreType.DMA((len(parts), bits)),
            pltpu.SemaphoreType.DMA((len(parts), bits)),
        ],
        compiler_params=pltpu.CompilerParams(
            collective_id=1, has_side_effects=True, vmem_limit_bytes=63 * 2**20
        ),
    )(*grads)
    offset = (lax.axis_index("dp") * share) % D
    return lax.dynamic_slice(total.reshape(-1), (offset,), (share,))


def token_sum(left, right):
    return lax.dot_general(
        left, right, (((0,), (0,)), ((), ())), preferred_element_type=jnp.float32
    )


def times_t(left, right):
    return lax.dot_general(
        left, right, (((1,), (1,)), ((), ())), preferred_element_type=jnp.float32
    )


def layer_norm(values):
    center = values - jnp.mean(values, axis=-1, keepdims=True)
    factor = lax.rsqrt(jnp.mean(center * center, axis=-1, keepdims=True) + 1e-06)
    return (center * factor, factor)


def norm_back(grad_hat, normed, factor):
    return factor * (
        grad_hat
        - jnp.mean(grad_hat, axis=-1, keepdims=True)
        - normed * jnp.mean(grad_hat * normed, axis=-1, keepdims=True)
    )


PAD = -(-SEQ // 16) * 16
DEEP = D // HEADS


def dot(left, right):
    return lax.dot_general(
        left, right, (((1,), (0,)), ((), ())), preferred_element_type=jnp.float32
    )


def column_sum(values):
    return jnp.sum(values, axis=0, keepdims=True)


def block_kernel(
    images,
    tokens,
    cotangent,
    w_qkv,
    w_out,
    w_up,
    w_down,
    tail,
    result,
    grad_tokens,
    g_qkv,
    g_out,
    g_up,
    g_down,
    g_tail,
    x,
    dy,
    xhat,
    mid,
    a16,
    c16,
    q16,
    k16,
    v16,
    o16,
    probs,
    wide,
    slope,
    act16,
    du16,
    dh,
    do16,
    dqkv,
    dqkv16,
):
    rows = images * PAD
    bf16 = jnp.bfloat16
    for image in range(images):
        for here, there in ((x, tokens), (dy, cotangent)):
            begin = image * PAD
            last = SEQ // 8 * 8
            here[begin + last : begin + PAD, :] = jnp.zeros((PAD - last, D), jnp.float32)
            here[begin : begin + SEQ, :] = there[:, image, :]
    normed, factor_in = layer_norm(x[...])
    xhat[...] = normed
    a16[...] = (normed * tail[0:1, :] + tail[1:2, :]).astype(bf16)
    q16[...] = (dot(a16[...], w_qkv[:, 0:D]) + tail[2:3, :]).astype(bf16)
    k16[...] = dot(a16[...], w_qkv[:, D : 2 * D]).astype(bf16)
    v16[...] = (dot(a16[...], w_qkv[:, 2 * D :]) + tail[3:4, :]).astype(bf16)
    scale = DEEP ** (-0.5)
    inside = lax.broadcasted_iota(jnp.int32, (PAD, PAD), 1) < SEQ

    def attend(image, carry):
        span = pl.ds(pl.multiple_of(image * PAD, 16), PAD)
        for head in range(HEADS):
            at = slice(head * DEEP, (head + 1) * DEEP)
            scores = times_t(q16[span, at], k16[span, at]) * scale
            scores = jnp.where(inside, scores, -1e30)
            raw = jnp.exp(scores - jnp.max(scores, axis=-1, keepdims=True))
            full = raw / jnp.sum(raw, axis=-1, keepdims=True)
            probs[image, head] = full
            o16[span, at] = dot(full.astype(bf16), v16[span, at]).astype(bf16)
        return carry

    lax.fori_loop(0, images, attend, 0)
    hidden = x[...] + (dot(o16[...], w_out[...]) + tail[4:5, :])
    x[...] = hidden
    normed, factor_mid = layer_norm(hidden)
    mid[...] = normed
    c16[...] = (normed * tail[5:6, :] + tail[6:7, :]).astype(bf16)
    for column in range(FF // D):
        at = slice(column * D, (column + 1) * D)
        wide[:, at] = dot(c16[...], w_up[:, at]) + tail[8 + column : 9 + column, :]
    step = 16

    def gelu(index, carry):
        span = pl.ds(pl.multiple_of(index * step, step), step)
        pre = wide[span, :]
        phi = 0.5 * (1.0 + lax.erf(pre * 0.7071067811865476))
        act16[span, :] = (pre * phi).astype(bf16)
        slope[span, :] = phi + pre * jnp.exp(-0.5 * pre * pre) * 0.3989422804014327
        return carry

    lax.fori_loop(0, rows // step, gelu, 0)
    final = x[...] + (dot(act16[...], w_down[...]) + tail[7:8, :])
    for image in range(images):
        result[:, image, :] = final[image * PAD : image * PAD + SEQ, :]

    dy16 = dy[...].astype(bf16)
    g_down[...] = token_sum(act16[...], dy16)
    g_tail[7:8, :] = column_sum(dy[...])
    wide[...] = times_t(dy16, w_down[...])

    def grad_pre(index, total):
        span = pl.ds(pl.multiple_of(index * step, step), step)
        value = wide[span, :] * slope[span, :]
        du16[span, :] = value.astype(bf16)
        return total + value

    total = lax.fori_loop(0, rows // step, grad_pre, jnp.zeros((step, FF), jnp.float32))
    total = column_sum(total)
    for column in range(FF // D):
        g_tail[8 + column : 9 + column, :] = total[:, column * D : (column + 1) * D]
    g_tail[12:16, :] = jnp.zeros((4, D), jnp.float32)
    g_up[...] = token_sum(c16[...], du16[...])
    grad_mlp = times_t(du16[...], w_up[...])
    g_tail[5:6, :] = column_sum(grad_mlp * mid[...])
    g_tail[6:7, :] = column_sum(grad_mlp)
    grad_hidden = dy[...] + norm_back(grad_mlp * tail[5:6, :], mid[...], factor_mid)
    dh[...] = grad_hidden
    g_tail[4:5, :] = column_sum(grad_hidden)
    dh16 = grad_hidden.astype(bf16)
    g_out[...] = token_sum(o16[...], dh16)
    do16[...] = times_t(dh16, w_out[...]).astype(bf16)

    def attend_back(image, carry):
        span = pl.ds(pl.multiple_of(image * PAD, 16), PAD)
        for head in range(HEADS):
            at = slice(head * DEEP, (head + 1) * DEEP)
            full = probs[image, head]
            grad_o = do16[span, at]
            dqkv[span, 2 * D + head * DEEP : 2 * D + (head + 1) * DEEP] = token_sum(
                full.astype(bf16), grad_o
            )
            grad_probs = times_t(grad_o, v16[span, at])
            delta = jnp.sum(full * grad_probs, axis=-1, keepdims=True)
            grad_scores = (full * (grad_probs - delta) * scale).astype(bf16)
            dqkv[span, at] = dot(grad_scores, k16[span, at])
            dqkv[span, D + head * DEEP : D + (head + 1) * DEEP] = token_sum(
                grad_scores, q16[span, at]
            )
        return carry

    lax.fori_loop(0, images, attend_back, 0)
    g_tail[2:3, :] = column_sum(dqkv[:, 0:D])
    g_tail[3:4, :] = column_sum(dqkv[:, 2 * D :])
    dqkv16[...] = dqkv[...].astype(bf16)
    g_qkv[...] = token_sum(a16[...], dqkv16[...])
    grad_in = times_t(dqkv16[...], w_qkv[...])
    g_tail[0:1, :] = column_sum(grad_in * xhat[...])
    g_tail[1:2, :] = column_sum(grad_in)
    final = dh[...] + norm_back(grad_in * tail[0:1, :], xhat[...], factor_in)
    for image in range(images):
        grad_tokens[:, image, :] = final[image * PAD : image * PAD + SEQ, :]


def block_scratch(images):
    rows = images * PAD
    f32, bf16 = jnp.float32, jnp.bfloat16
    return [
        pltpu.VMEM(shape, kind)
        for shape, kind in (
            ((rows, D), f32),
            ((rows, D), f32),
            ((rows, D), f32),
            ((rows, D), f32),
            ((rows, D), bf16),
            ((rows, D), bf16),
            ((rows, D), bf16),
            ((rows, D), bf16),
            ((rows, D), bf16),
            ((rows, D), bf16),
            ((images, HEADS, PAD, PAD), f32),
            ((rows, FF), f32),
            ((rows, FF), f32),
            ((rows, FF), bf16),
            ((rows, FF), bf16),
            ((rows, D), f32),
            ((rows, D), bf16),
            ((rows, 3 * D), f32),
            ((rows, 3 * D), bf16),
        )
    ]


def block(tokens, cotangent, weights):
    images = tokens.shape[1]
    f32 = jnp.float32
    vmem = pl.BlockSpec(memory_space=pltpu.VMEM)
    return pl.pallas_call(
        functools.partial(block_kernel, images),
        out_shape=tuple(
            jax.ShapeDtypeStruct(shape, f32)
            for shape in (
                tokens.shape,
                tokens.shape,
                (D, 3 * D),
                (D, D),
                (D, FF),
                (FF, D),
                (16, D),
            )
        ),
        in_specs=[vmem] * 7,
        out_specs=[vmem] * 7,
        scratch_shapes=block_scratch(images),
        compiler_params=pltpu.CompilerParams(vmem_limit_bytes=63 * 2**20),
    )(tokens, cotangent, *weights)


def adamw(params, grads, first, second, position):
    first_end = 3 * D * D
    second_end = first_end + D * D
    third_end = second_end + D * FF
    fourth_end = third_end + FF * D
    rate = jnp.where(
        position < first_end,
        0.01,
        jnp.where(
            position < second_end,
            0.1,
            jnp.where(position < third_end, 0.01, jnp.where(position < fourth_end, 0.005, 0.1)),
        ),
    )
    first_new = 0.9 * first + 0.1 * grads
    second_new = 0.999 * second + 0.001 * grads * grads
    update = (
        first_new / (1.0 - 0.9**STEP) / (jnp.sqrt(second_new / (1.0 - 0.999**STEP)) + 1e-08)
        + 0.1 * params
    )
    return (params - rate * update, first_new, second_new)


def per_device(tokens, params, moment1, moment2, cotangent):
    devices = lax.axis_size("dp")
    length = params.shape[0]
    weights = gather_weights(params, devices)
    result, grad_tokens, *grads = block(
        tokens.transpose(1, 0, 2), cotangent.transpose(1, 0, 2), weights
    )
    result, grad_tokens = result.transpose(1, 0, 2), grad_tokens.transpose(1, 0, 2)
    shares = scatter_grads(grads, devices, length)
    count = tokens.shape[0] * tokens.shape[1] * devices
    grad_params = shares * (1.0 / math.sqrt(count))
    position = lax.axis_index("dp") * length + jnp.arange(length, dtype=jnp.int32)
    new_params, new_first, new_second = adamw(params, grad_params, moment1, moment2, position)
    return (result, grad_tokens, grad_params, new_params, new_first, new_second)


def solution(mesh):
    in_specs = (P("dp", None, None), P("dp"), P("dp"), P("dp"), P("dp", None, None))
    out_specs = (P("dp", None, None), P("dp", None, None), P("dp"), P("dp"), P("dp"), P("dp"))
    return jax.shard_map(
        per_device, mesh=mesh, in_specs=in_specs, out_specs=out_specs, check_vma=False
    )
```

```python
import math

import jax
import jax.numpy as jnp
from jax import lax
from jax.experimental import pallas as pl
from jax.experimental.pallas import tpu as pltpu
import functools
from jax.sharding import PartitionSpec as P

D = 384
HEADS = 6
FF = 1536
SEQ = 197
STEP = 3


LANES = 128
LINES = 4 * 1152 + 12


def plan(devices, share):
    bits = devices.bit_length() - 1
    rows = -(-(share + D - 1) // D)
    rows = -(-rows // 32) * 32
    far = list(range(bits - 1, 2, -1))
    orders = [far + [1, 2, 0], far + [2, 1, 0], [1, 2] + far + [0], [2, 1] + far + [0]]
    half = rows // 2
    if half % 16 == 0 and half > 16:
        sizes = [half - 16, half - 16, 16, 16]
    else:
        sizes = [half, half]
    parts = []
    start = 0
    for index, size in enumerate(sizes):
        parts.append((start, size, orders[index]))
        start += size
    return bits, rows, parts


def place(device, order):
    spot = 0
    for index, bit in enumerate(order):
        spot = spot + ((device // 2**bit) % 2) * 2**index
    return spot


def other(device, bit):
    step = 2**bit
    return device + step - 2 * step * ((device // step) % 2)


def greet(me, bits):
    barrier = pltpu.get_barrier_semaphore()
    for bit in range(bits):
        pl.semaphore_signal(
            barrier, inc=1, device_id=(other(me, bit),), device_id_type=pl.DeviceIdType.MESH
        )
    pl.semaphore_wait(barrier, bits)


def gather_kernel(devices, share, shard, w_qkv, w_out, w_up, w_down, tail, lines, *rest):
    bits, rows, parts = plan(devices, share)
    slots = rest[: len(parts)]
    local_sem, send_sem, recv_sem = rest[len(parts) :]
    me = lax.axis_index("dp")
    own = []
    for index, (start, size, order) in enumerate(parts):
        copy = pltpu.make_async_copy(
            shard.at[pl.ds(start, size)], slots[index].at[place(me, order)], local_sem.at[index]
        )
        copy.start()
        own.append(copy)
    greet(me, bits)
    for copy in own:
        copy.wait()
    waiting = [None] * len(parts)
    for stage in range(bits):
        for index, (start, size, order) in enumerate(parts):
            if waiting[index] is not None:
                waiting[index].wait()
            block = 2**stage
            begin = (place(me, order) // block) * block
            piece = slots[index].at[pl.ds(begin, block)]
            copy = pltpu.make_async_remote_copy(
                src_ref=piece,
                dst_ref=piece,
                send_sem=send_sem.at[index, stage],
                recv_sem=recv_sem.at[index, stage],
                device_id=(other(me, order[stage]),),
                device_id_type=pl.DeviceIdType.MESH,
            )
            copy.start()
            waiting[index] = copy
    for copy in waiting:
        copy.wait()
    chunks = D // LANES
    for device in range(devices):
        first = device * share // D
        shared = device * share % D != 0
        for index, (start, size, order) in enumerate(parts):
            spot = place(device, order)
            at = first + start
            for chunk in range(chunks):
                if start == 0 and shared:
                    before = lines[chunk, at : at + 1, :]
                lines[chunk, at : at + size, :] = slots[index][
                    spot, :, chunk * LANES : (chunk + 1) * LANES
                ].astype(jnp.float32)
                if start == 0 and shared:
                    lines[chunk, at : at + 1, :] = lines[chunk, at : at + 1, :] + before
    spread(lines, 0, w_qkv, 3)
    spread(lines, 1152, w_out, 1)
    spread(lines, 1536, w_up, 4)
    spread(lines, 3072, w_down, 1)
    spread(lines, 4608, tail, 1)


def spread(lines, first, out, times):
    height = out.shape[0]
    for column in range(times):
        for chunk in range(D // LANES):
            if times == 1:
                value = lines[chunk, first : first + height, :]
            else:
                value = lines[chunk, pl.ds(first + column, height, stride=times), :]
            at = column * D + chunk * LANES
            out[:, at : at + LANES] = value.astype(out.dtype)


def gather_weights(params, devices):
    share = params.shape[0]
    bits, rows, parts = plan(devices, share)
    offset = (lax.axis_index("dp") * share) % D
    flat = jnp.zeros((rows * D,), jnp.float32)
    flat = lax.dynamic_update_slice(flat, params, (offset,))
    shard = flat.reshape(rows, D).astype(jnp.bfloat16)
    vmem = pl.BlockSpec(memory_space=pltpu.VMEM)
    return pl.pallas_call(
        functools.partial(gather_kernel, devices, share),
        out_shape=(
            jax.ShapeDtypeStruct((D, 3 * D), jnp.bfloat16),
            jax.ShapeDtypeStruct((D, D), jnp.bfloat16),
            jax.ShapeDtypeStruct((D, FF), jnp.bfloat16),
            jax.ShapeDtypeStruct((FF, D), jnp.bfloat16),
            jax.ShapeDtypeStruct((16, D), jnp.float32),
        ),
        in_specs=[vmem],
        out_specs=[vmem] * 5,
        scratch_shapes=[pltpu.VMEM((D // LANES, LINES + rows + 24, LANES), jnp.float32)]
        + [pltpu.VMEM((devices, size, D), jnp.bfloat16) for _, size, _ in parts]
        + [
            pltpu.SemaphoreType.DMA((len(parts),)),
            pltpu.SemaphoreType.DMA((len(parts), bits)),
            pltpu.SemaphoreType.DMA((len(parts), bits)),
        ],
        compiler_params=pltpu.CompilerParams(
            collective_id=0, has_side_effects=True, vmem_limit_bytes=60 * 2**20
        ),
    )(shard)


def scatter_kernel(devices, share, g_qkv, g_out, g_up, g_down, g_tail, out, lines, *rest):
    bits, rows, parts = plan(devices, share)
    count = len(parts)
    slots, landed, sums = rest[:count], rest[count : 2 * count], rest[2 * count : 3 * count]
    send_sem, recv_sem = rest[3 * count :]
    me = lax.axis_index("dp")
    collect(lines, 0, g_qkv, 3)
    collect(lines, 1152, g_out, 1)
    collect(lines, 1536, g_up, 4)
    collect(lines, 3072, g_down, 1)
    collect(lines, 4608, g_tail, 1)
    lines[:, 4624:, :] = jnp.zeros_like(lines[:, 4624:, :])

    def pack(index):
        start, size, order = parts[index]
        for device in range(devices):
            spot = place(device, order)
            at = device * share // D + start
            for chunk in range(D // LANES):
                slots[index][spot, :, chunk * LANES : (chunk + 1) * LANES] = lines[
                    chunk, at : at + size, :
                ].astype(jnp.bfloat16)

    greet(me, bits)
    waiting = [None] * count

    def send(index, stage):
        order = parts[index][2]
        block = 2**stage
        spot = place(me, order) // block
        away = spot + 1 - 2 * (spot % 2)
        copy = pltpu.make_async_remote_copy(
            src_ref=slots[index].at[pl.ds(away * block, block)],
            dst_ref=landed[index].at[pl.ds(block - 1, block)],
            send_sem=send_sem.at[index, stage],
            recv_sem=recv_sem.at[index, stage],
            device_id=(other(me, order[stage]),),
            device_id_type=pl.DeviceIdType.MESH,
        )
        copy.start()
        return copy

    for index in range(count):
        pack(index)
        waiting[index] = send(index, bits - 1)
    for stage in range(bits - 1, -1, -1):
        for index, (start, size, order) in enumerate(parts):
            waiting[index].wait()
            block = 2**stage
            begin = (place(me, order) // block) * block
            if stage == 0:
                piece = sums[index][begin] if bits > 1 else slots[index][begin].astype(jnp.float32)
                out[start : start + size, :] = piece + landed[index][0].astype(jnp.float32)
                continue

            def add(step, carry, index=index, begin=begin, block=block, stage=stage):
                spot = begin + step
                if stage == bits - 1:
                    old = slots[index][spot].astype(jnp.float32)
                else:
                    old = sums[index][spot]
                new = old + landed[index][block - 1 + step].astype(jnp.float32)
                sums[index][spot] = new
                slots[index][spot] = new.astype(jnp.bfloat16)
                return carry

            lax.fori_loop(0, block, add, 0)
            waiting[index] = send(index, stage - 1)


def collect(lines, first, grads, times):
    height = grads.shape[0]
    for column in range(times):
        for chunk in range(D // LANES):
            at = column * D + chunk * LANES
            value = grads[:, at : at + LANES]
            if times == 1:
                lines[chunk, first : first + height, :] = value
            else:
                lines[chunk, pl.ds(first + column, height, stride=times), :] = value


def scatter_grads(grads, devices, share):
    bits, rows, parts = plan(devices, share)
    vmem = pl.BlockSpec(memory_space=pltpu.VMEM)
    total = pl.pallas_call(
        functools.partial(scatter_kernel, devices, share),
        out_shape=jax.ShapeDtypeStruct((rows, D), jnp.float32),
        in_specs=[vmem] * 5,
        out_specs=vmem,
        scratch_shapes=[pltpu.VMEM((D // LANES, LINES + rows + 24, LANES), jnp.float32)]
        + [pltpu.VMEM((devices, size, D), jnp.bfloat16) for _, size, _ in parts]
        + [pltpu.VMEM((devices, size, D), jnp.bfloat16) for _, size, _ in parts]
        + [pltpu.VMEM((devices, size, D), jnp.float32) for _, size, _ in parts]
        + [
            pltpu.SemaphoreType.DMA((len(parts), bits)),
            pltpu.SemaphoreType.DMA((len(parts), bits)),
        ],
        compiler_params=pltpu.CompilerParams(
            collective_id=1, has_side_effects=True, vmem_limit_bytes=63 * 2**20
        ),
    )(*grads)
    offset = (lax.axis_index("dp") * share) % D
    return lax.dynamic_slice(total.reshape(-1), (offset,), (share,))


def token_sum(left, right):
    return lax.dot_general(
        left, right, (((0,), (0,)), ((), ())), preferred_element_type=jnp.float32
    )


def times_t(left, right):
    return lax.dot_general(
        left, right, (((1,), (1,)), ((), ())), preferred_element_type=jnp.float32
    )


def layer_norm(values):
    center = values - jnp.mean(values, axis=-1, keepdims=True)
    factor = lax.rsqrt(jnp.mean(center * center, axis=-1, keepdims=True) + 1e-06)
    return (center * factor, factor)


def norm_back(grad_hat, normed, factor):
    return factor * (
        grad_hat
        - jnp.mean(grad_hat, axis=-1, keepdims=True)
        - normed * jnp.mean(grad_hat * normed, axis=-1, keepdims=True)
    )


PAD = -(-SEQ // 16) * 16
DEEP = D // HEADS


def dot(left, right):
    return lax.dot_general(
        left, right, (((1,), (0,)), ((), ())), preferred_element_type=jnp.float32
    )


def column_sum(values):
    return jnp.sum(values, axis=0, keepdims=True)


def block_kernel(
    images,
    tokens,
    cotangent,
    w_qkv,
    w_out,
    w_up,
    w_down,
    tail,
    result,
    grad_tokens,
    g_qkv,
    g_out,
    g_up,
    g_down,
    g_tail,
    x,
    dy,
    xhat,
    mid,
    a16,
    c16,
    q16,
    k16,
    v16,
    o16,
    probs,
    wide,
    slope,
    act16,
    du16,
    dh,
    do16,
    dqkv,
    dqkv16,
):
    rows = images * PAD
    bf16 = jnp.bfloat16
    for image in range(images):
        for here, there in ((x, tokens), (dy, cotangent)):
            begin = image * PAD
            last = SEQ // 8 * 8
            here[begin + last : begin + PAD, :] = jnp.zeros((PAD - last, D), jnp.float32)
            here[begin : begin + SEQ, :] = there[:, image, :]
    normed, factor_in = layer_norm(x[...])
    xhat[...] = normed
    a16[...] = (normed * tail[0:1, :] + tail[1:2, :]).astype(bf16)
    q16[...] = (dot(a16[...], w_qkv[:, 0:D]) + tail[2:3, :]).astype(bf16)
    k16[...] = dot(a16[...], w_qkv[:, D : 2 * D]).astype(bf16)
    v16[...] = (dot(a16[...], w_qkv[:, 2 * D :]) + tail[3:4, :]).astype(bf16)
    scale = DEEP ** (-0.5)
    inside = lax.broadcasted_iota(jnp.int32, (PAD, PAD), 1) < SEQ

    def attend(image, carry):
        span = pl.ds(pl.multiple_of(image * PAD, 16), PAD)
        for head in range(HEADS):
            at = slice(head * DEEP, (head + 1) * DEEP)
            scores = times_t(q16[span, at], k16[span, at]) * scale
            scores = jnp.where(inside, scores, -1e30)
            raw = jnp.exp(scores - jnp.max(scores, axis=-1, keepdims=True))
            full = raw / jnp.sum(raw, axis=-1, keepdims=True)
            probs[image, head] = full
            o16[span, at] = dot(full.astype(bf16), v16[span, at]).astype(bf16)
        return carry

    lax.fori_loop(0, images, attend, 0)
    hidden = x[...] + (dot(o16[...], w_out[...]) + tail[4:5, :])
    x[...] = hidden
    normed, factor_mid = layer_norm(hidden)
    mid[...] = normed
    c16[...] = (normed * tail[5:6, :] + tail[6:7, :]).astype(bf16)
    for column in range(FF // D):
        at = slice(column * D, (column + 1) * D)
        wide[:, at] = dot(c16[...], w_up[:, at]) + tail[8 + column : 9 + column, :]
    step = 16

    def gelu(index, carry):
        span = pl.ds(pl.multiple_of(index * step, step), step)
        pre = wide[span, :]
        phi = 0.5 * (1.0 + lax.erf(pre * 0.7071067811865476))
        act16[span, :] = (pre * phi).astype(bf16)
        slope[span, :] = phi + pre * jnp.exp(-0.5 * pre * pre) * 0.3989422804014327
        return carry

    lax.fori_loop(0, rows // step, gelu, 0)
    final = x[...] + (dot(act16[...], w_down[...]) + tail[7:8, :])
    for image in range(images):
        result[:, image, :] = final[image * PAD : image * PAD + SEQ, :]

    dy16 = dy[...].astype(bf16)
    g_down[...] = token_sum(act16[...], dy16)
    g_tail[7:8, :] = column_sum(dy[...])
    wide[...] = times_t(dy16, w_down[...])

    def grad_pre(index, total):
        span = pl.ds(pl.multiple_of(index * step, step), step)
        value = wide[span, :] * slope[span, :]
        du16[span, :] = value.astype(bf16)
        return total + value

    total = lax.fori_loop(0, rows // step, grad_pre, jnp.zeros((step, FF), jnp.float32))
    total = column_sum(total)
    for column in range(FF // D):
        g_tail[8 + column : 9 + column, :] = total[:, column * D : (column + 1) * D]
    g_tail[12:16, :] = jnp.zeros((4, D), jnp.float32)
    g_up[...] = token_sum(c16[...], du16[...])
    grad_mlp = times_t(du16[...], w_up[...])
    g_tail[5:6, :] = column_sum(grad_mlp * mid[...])
    g_tail[6:7, :] = column_sum(grad_mlp)
    grad_hidden = dy[...] + norm_back(grad_mlp * tail[5:6, :], mid[...], factor_mid)
    dh[...] = grad_hidden
    g_tail[4:5, :] = column_sum(grad_hidden)
    dh16 = grad_hidden.astype(bf16)
    g_out[...] = token_sum(o16[...], dh16)
    do16[...] = times_t(dh16, w_out[...]).astype(bf16)

    def attend_back(image, carry):
        span = pl.ds(pl.multiple_of(image * PAD, 16), PAD)
        for head in range(HEADS):
            at = slice(head * DEEP, (head + 1) * DEEP)
            full = probs[image, head]
            grad_o = do16[span, at]
            dqkv[span, 2 * D + head * DEEP : 2 * D + (head + 1) * DEEP] = token_sum(
                full.astype(bf16), grad_o
            )
            grad_probs = times_t(grad_o, v16[span, at])
            delta = jnp.sum(full * grad_probs, axis=-1, keepdims=True)
            grad_scores = (full * (grad_probs - delta) * scale).astype(bf16)
            dqkv[span, at] = dot(grad_scores, k16[span, at])
            dqkv[span, D + head * DEEP : D + (head + 1) * DEEP] = token_sum(
                grad_scores, q16[span, at]
            )
        return carry

    lax.fori_loop(0, images, attend_back, 0)
    g_tail[2:3, :] = column_sum(dqkv[:, 0:D])
    g_tail[3:4, :] = column_sum(dqkv[:, 2 * D :])
    dqkv16[...] = dqkv[...].astype(bf16)
    g_qkv[...] = token_sum(a16[...], dqkv16[...])
    grad_in = times_t(dqkv16[...], w_qkv[...])
    g_tail[0:1, :] = column_sum(grad_in * xhat[...])
    g_tail[1:2, :] = column_sum(grad_in)
    final = dh[...] + norm_back(grad_in * tail[0:1, :], xhat[...], factor_in)
    for image in range(images):
        grad_tokens[:, image, :] = final[image * PAD : image * PAD + SEQ, :]


def block_scratch(images):
    rows = images * PAD
    f32, bf16 = jnp.float32, jnp.bfloat16
    return [
        pltpu.VMEM(shape, kind)
        for shape, kind in (
            ((rows, D), f32),
            ((rows, D), f32),
            ((rows, D), f32),
            ((rows, D), f32),
            ((rows, D), bf16),
            ((rows, D), bf16),
            ((rows, D), bf16),
            ((rows, D), bf16),
            ((rows, D), bf16),
            ((rows, D), bf16),
            ((images, HEADS, PAD, PAD), f32),
            ((rows, FF), f32),
            ((rows, FF), f32),
            ((rows, FF), bf16),
            ((rows, FF), bf16),
            ((rows, D), f32),
            ((rows, D), bf16),
            ((rows, 3 * D), f32),
            ((rows, 3 * D), bf16),
        )
    ]


def block(tokens, cotangent, weights):
    images = tokens.shape[1]
    f32 = jnp.float32
    vmem = pl.BlockSpec(memory_space=pltpu.VMEM)
    return pl.pallas_call(
        functools.partial(block_kernel, images),
        out_shape=tuple(
            jax.ShapeDtypeStruct(shape, f32)
            for shape in (
                tokens.shape,
                tokens.shape,
                (D, 3 * D),
                (D, D),
                (D, FF),
                (FF, D),
                (16, D),
            )
        ),
        in_specs=[vmem] * 7,
        out_specs=[vmem] * 7,
        scratch_shapes=block_scratch(images),
        compiler_params=pltpu.CompilerParams(vmem_limit_bytes=63 * 2**20),
    )(tokens, cotangent, *weights)


def adamw(params, grads, first, second, position):
    first_end = 3 * D * D
    second_end = first_end + D * D
    third_end = second_end + D * FF
    fourth_end = third_end + FF * D
    rate = jnp.where(
        position < first_end,
        0.01,
        jnp.where(
            position < second_end,
            0.1,
            jnp.where(position < third_end, 0.01, jnp.where(position < fourth_end, 0.005, 0.1)),
        ),
    )
    first_new = 0.9 * first + 0.1 * grads
    second_new = 0.999 * second + 0.001 * grads * grads
    update = (
        first_new / (1.0 - 0.9**STEP) / (jnp.sqrt(second_new / (1.0 - 0.999**STEP)) + 1e-08)
        + 0.1 * params
    )
    return (params - rate * update, first_new, second_new)


def per_device(tokens, params, moment1, moment2, cotangent):
    devices = lax.axis_size("dp")
    length = params.shape[0]
    weights = gather_weights(params, devices)
    result, grad_tokens, *grads = block(
        tokens.transpose(1, 0, 2), cotangent.transpose(1, 0, 2), weights
    )
    result, grad_tokens = result.transpose(1, 0, 2), grad_tokens.transpose(1, 0, 2)
    shares = scatter_grads(grads, devices, length)
    count = tokens.shape[0] * tokens.shape[1] * devices
    grad_params = shares * (1.0 / math.sqrt(count))
    position = lax.axis_index("dp") * length + jnp.arange(length, dtype=jnp.int32)
    new_params, new_first, new_second = adamw(params, grad_params, moment1, moment2, position)
    return (result, grad_tokens, grad_params, new_params, new_first, new_second)


def solution(mesh):
    in_specs = (P("dp", None, None), P("dp"), P("dp"), P("dp"), P("dp", None, None))
    out_specs = (P("dp", None, None), P("dp", None, None), P("dp"), P("dp"), P("dp"), P("dp"))
    return jax.shard_map(
        per_device, mesh=mesh, in_specs=in_specs, out_specs=out_specs, check_vma=False
    )
```
